32 devices in a mesh: dp: 32 (over z, y, x, core).
Axes of the slice: x: 2, y: 2, z: 4, core: 2. Of those that a mesh axis runs over, the one named last changes fastest.
Arguments:
- patches: bfloat16 [32768, 1664], P('dp')
- ln_gain: float32 [1664], replicated, may hold values from 0.25 to 1.75
- w_qkv: bfloat16 [1664, 2496], P('dp')
- w_out: bfloat16 [832, 1664], P(None, 'dp'), may hold values from -0.21875 to 0.21875
- w_proj: bfloat16 [6656, 2048], P('dp'), may hold values from -0.078125 to 0.078125
- seg_ids: int32 [32768], P('dp'), may hold values from 0 to 4, as said below
- patch_mask: int32 [32768], P('dp'), may hold values 0 or 1
- grid_hw: int32 [128, 2], P('dp'), may hold values from 12 to 16, as said below
- owners: int32 [128], P('dp'), may hold values from 0 to 31
Outputs:
- routed: bfloat16 [8192, 2048], P('dp')
- image_rms: float32 [128], P('dp')
- image_max_logit: float32 [128], P('dp')
The draws below stay inside these ranges and needn't reach their ends.
Inputs may be any that keep to these rules, and one draw needn't show every extreme that they name: `seg_ids`: within each pack the images' tokens lie in order without gaps from the pack's first token, each image taking grid height times width consecutive tokens with segment numbers 0 to 3; the remaining tokens carry 4. `grid_hw`: heights and widths are 12, 14 or 16; every pack has an image of 16 x 16 patches, so an image has at most 64 merged rows, and every pack also has an image of height 12.
All inputs are finite; a program needn't handle non-finite values. No bound on the sum of `patch_mask` on one device may be relied on, other than what follows from the above.
Results may differ from the reference program's by a relative error of at most 0.006.
Values may be sent and summed in bfloat16 or wider, within the bound.
A program may use at most 192 MiB of HBM per device.

```python
import jax
import jax.numpy as jnp
from jax import lax

D = 1664
HEADS = 8
HEAD_DIM = 104
PROJ = 2048
TOK_DEV = 1024
CAP = 64
HW = 832
REQ_DEV = 4
WRAPS = 2
TOKENS = 32768
REQS = 128
N_DP = 32


def draw_patches(key, part):
    first_key = jax.random.fold_in(key, 0)
    values = jax.random.normal(first_key, (TOKENS, D), jnp.float32)
    return jnp.clip(values, -6.0, 6.0).astype(jnp.bfloat16)


def draw_w_qkv(key, part):
    hidden_w = HEADS * HEAD_DIM
    first_key = jax.random.fold_in(key, 0)
    base = jax.random.normal(first_key, (D, 3 * hidden_w), jnp.float32) * D ** (-0.5)
    return base.astype(jnp.bfloat16)


def image_layout(key):
    packs = REQS // REQ_DEV
    keys_all = jax.random.split(key, 3)
    side_h = 12 + 2 * jax.random.randint(keys_all[0], (packs, REQ_DEV), 0, 3)
    side_w = 12 + 2 * jax.random.randint(keys_all[1], (packs, REQ_DEV), 0, 3)
    biggest = jax.random.randint(keys_all[2], (packs, 1), 0, REQ_DEV)
    image_idx = jnp.arange(REQ_DEV, dtype=jnp.int32)[None, :]
    forced = image_idx == biggest
    shorter = image_idx == (biggest + 1) % REQ_DEV
    heights = jnp.where(forced, 16, jnp.where(shorter, 12, side_h)).astype(jnp.int32)
    widths = jnp.where(forced, 16, side_w).astype(jnp.int32)
    return (heights, widths)


def draw_grid_hw(key, part):
    heights, widths = image_layout(jax.random.fold_in(key, 11))
    return jnp.stack([heights, widths], axis=-1).reshape(REQS, 2).astype(jnp.int32)


def draw_seg_ids(key, part):
    heights, widths = image_layout(jax.random.fold_in(key, 11))
    areas = (heights * widths).astype(jnp.int32)
    ends_at = jnp.cumsum(areas, axis=1).astype(jnp.int32)
    position = jnp.arange(TOK_DEV, dtype=jnp.int32)
    seg_vals = jnp.sum((position[None, :, None] >= ends_at[:, None, :]).astype(jnp.int32), axis=2)
    return seg_vals.reshape(TOKENS).astype(jnp.int32)


def with_ends(drawn, stream_key, least, top_value):
    longest = drawn.shape.index(max(drawn.shape))
    spots = []
    for shift in (0, 1):
        where = [jax.random.randint(jax.random.fold_in(stream_key, axis), (), 0, length) for axis, length in enumerate(drawn.shape)]
        where[longest] = (where[longest] + shift) % drawn.shape[longest]
        spots.append(tuple(where))
    return drawn.at[spots[0]].set(least).at[spots[1]].set(top_value)


def level_of(rng, extent, cuts, least, largest):
    def one(axis_at, parts):
        steps = jax.random.uniform(jax.random.fold_in(jax.random.fold_in(rng, 6), axis_at), (parts,), jnp.float32, least / len(cuts), largest / len(cuts))
        return jnp.repeat(jnp.exp(steps), extent[axis_at] // parts).reshape((-1,) + (1,) * (len(extent) - axis_at - 1))

    factor_of = one(*cuts[0])
    for cut in cuts[1:]:
        factor_of = factor_of * one(*cut)
    return factor_of


def scatter_about(stream_key, shape, deviation, reach, cuts=(), kind=jnp.bfloat16):
    values = jax.random.normal(stream_key, shape, jnp.float32) * deviation
    if len(cuts) > 0:
        values = level_of(stream_key, shape, cuts, -0.22, 0.18) * values
    return jnp.clip(values, min=-reach, max=reach).astype(kind)


def setup_inputs(seed: int = 0) -> dict:
    key_list = jax.random.split(jax.random.key(seed), 10)
    patches = draw_patches(jax.random.fold_in(key_list[9], 71), 0)
    ln_gain = jnp.clip(1.0 + 0.15 * jax.random.normal(key_list[1], (D,), jnp.float32), 0.25, 1.75)
    w_qkv = draw_w_qkv(jax.random.fold_in(key_list[9], 71), 0)
    w_out = scatter_about(key_list[3], (HW, D), HW ** -0.5, 0.21875, ((1, 32),))
    w_proj = scatter_about(key_list[4], (4 * D, PROJ), (4 * D) ** -0.5, 0.078125, ((0, 32),))
    seg_ids = draw_seg_ids(jax.random.fold_in(key_list[9], 71), 0)
    patch_mask = with_ends((jax.random.randint(key_list[6], (TOKENS,), 0, 8) < 7).astype(jnp.int32), jax.random.fold_in(key_list[6], 1), 0, 1)
    grid_hw = draw_grid_hw(jax.random.fold_in(key_list[9], 71), 0)
    owners = with_ends(jax.random.randint(key_list[8], (REQS,), 0, N_DP), jax.random.fold_in(key_list[8], 1), 0, N_DP - 1).astype(jnp.int32)
    return {"patches": patches, "ln_gain": ln_gain, "w_qkv": w_qkv, "w_out": w_out, "w_proj": w_proj, "seg_ids": seg_ids, "patch_mask": patch_mask, "grid_hw": grid_hw, "owners": owners}


def token_places(seg_row, grid_rows):
    heights = grid_rows[:, 0]
    widths = grid_rows[:, 1]
    areas = (heights * widths).astype(jnp.int32)
    ends_at = jnp.cumsum(areas).astype(jnp.int32)
    starts = (ends_at - areas).astype(jnp.int32)
    image_count = grid_rows.shape[0]
    member = seg_row[:, None] == jnp.arange(image_count, dtype=jnp.int32)[None, :]
    start_tok = lax.optimization_barrier(jnp.sum(jnp.where(member, starts[None, :], 0), axis=1)).astype(jnp.int32)
    half_w = jnp.maximum(lax.optimization_barrier(jnp.sum(jnp.where(member, (widths // 2)[None, :], 0), axis=1)), 1).astype(jnp.int32)
    offset = jnp.arange(seg_row.shape[0], dtype=jnp.int32) - start_tok
    window = offset // 4
    corner = offset % 4
    row_pos = 2 * (window // half_w) + corner // 2
    col_pos = 2 * (window % half_w) + corner % 2
    return (row_pos.astype(jnp.float32), col_pos.astype(jnp.float32), areas, starts)

def rotate(heads_in, row_pos, col_pos):
    quarter = heads_in.shape[-1] // 4
    theta = 100.0 ** (-jnp.arange(quarter, dtype=jnp.float32) / quarter)
    out_parts = []
    for which_pos, offset_at in ((row_pos, 0), (col_pos, 2 * quarter)):
        angles = (which_pos[:, None] * theta[None, :])[:, None, :]
        cosine = jnp.cos(angles)
        sine_val = jnp.sin(angles)
        part_a = heads_in[..., offset_at:offset_at + quarter]
        part_b = heads_in[..., offset_at + quarter:offset_at + 2 * quarter]
        out_parts += [part_a * cosine - part_b * sine_val, part_a * sine_val + part_b * cosine]
    return jnp.concatenate(out_parts, axis=-1)

def send_rows(proj_bf, starts, areas, owner_row, device_count):
    merged_rows = proj_bf.shape[0]
    wrap_count = (CAP + device_count - 1) // device_count
    dest_ids = jnp.arange(device_count, dtype=jnp.int32)[:, None, None]
    wrap_ids = jnp.arange(wrap_count, dtype=jnp.int32)[None, None, :]
    owner_here = owner_row.astype(jnp.int32)[None, :, None]
    row_within = (wrap_ids * device_count + (dest_ids - owner_here) % device_count).astype(jnp.int32)
    row_total = (areas // 4).astype(jnp.int32)[None, :, None]
    first_row = (starts // 4).astype(jnp.int32)[None, :, None]
    picked = jnp.where(row_within < row_total, first_row + row_within, merged_rows).astype(jnp.int32)
    padded = jnp.concatenate([proj_bf, jnp.zeros((1, proj_bf.shape[1]), proj_bf.dtype)], axis=0)
    return padded[picked]

def attend(queries, key_rows, values, seg_query, seg_key, mask_key):
    scores = jnp.einsum('qhd,khd->hqk', queries.astype(jnp.float32), key_rows.astype(jnp.float32)) * queries.shape[-1] ** (-0.5)
    query_idx = jnp.arange(queries.shape[0], dtype=jnp.int32)
    key_idx = jnp.arange(key_rows.shape[0], dtype=jnp.int32)
    allowed = (seg_query[:, None] == seg_key[None, :]) & ((mask_key[None, :] == 1) | (query_idx[:, None] == key_idx[None, :]))
    masked = jnp.where(allowed[None], scores, -1e+30)
    top_row = lax.optimization_barrier(jnp.max(masked, axis=-1, keepdims=True))
    expo = jnp.where(allowed[None], jnp.exp(masked - top_row), 0.0)
    weights = (expo / lax.optimization_barrier(jnp.sum(expo, axis=-1, keepdims=True))).astype(jnp.bfloat16)
    result = jnp.einsum('hqk,khd->qhd', weights.astype(jnp.float32), values.astype(jnp.float32)).astype(jnp.bfloat16)
    return (result.reshape(queries.shape[0], -1), lax.optimization_barrier(jnp.max(top_row[..., 0], axis=0)))

def reference(patches, ln_gain, w_qkv, w_out, w_proj, seg_ids, patch_mask, grid_hw, owners):
    packs = N_DP
    hidden_w = HEADS * HEAD_DIM

    def one_pack(inputs):
        tokens_in, seg_row, mask_row, grid_rows, owner_row = inputs
        tokens_f = tokens_in.astype(jnp.float32)
        mean_row = lax.optimization_barrier(jnp.mean(tokens_f, axis=-1, keepdims=True))
        centered = tokens_f - mean_row
        var_row = lax.optimization_barrier(jnp.mean(centered * centered, axis=-1, keepdims=True))
        normed = (centered * lax.rsqrt(var_row + 1e-06) * ln_gain).astype(jnp.bfloat16)
        mixed = jnp.dot(normed, w_qkv, preferred_element_type=jnp.float32)
        row_pos, col_pos, areas, starts = token_places(seg_row, grid_rows)
        shape_three = (TOK_DEV, HEADS, HEAD_DIM)
        queries = rotate(mixed[:, :hidden_w].reshape(shape_three), row_pos, col_pos).astype(jnp.bfloat16)
        key_rows = rotate(mixed[:, hidden_w:2 * hidden_w].reshape(shape_three), row_pos, col_pos).astype(jnp.bfloat16)
        values = mixed[:, 2 * hidden_w:].reshape(shape_three).astype(jnp.bfloat16)
        attended, row_top = attend(queries, key_rows, values, seg_row, seg_row, mask_row)
        member_q = seg_row[:, None] == jnp.arange(REQ_DEV, dtype=jnp.int32)[None, :]
        top_logit = lax.optimization_barrier(jnp.max(jnp.where(member_q, row_top[:, None], -1e+30), axis=0))
        residual = (tokens_f + jnp.dot(attended, w_out, preferred_element_type=jnp.float32)).astype(jnp.bfloat16)
        merged = residual.reshape(TOK_DEV // 4, 4 * D)
        projected = jnp.dot(merged, w_proj, preferred_element_type=jnp.float32)
        proj_bf = projected.astype(jnp.bfloat16)
        merged_seg = seg_row.reshape(-1, 4)[:, 0]
        member_m = merged_seg[:, None] == jnp.arange(REQ_DEV, dtype=jnp.int32)[None, :]
        squares = lax.optimization_barrier(jnp.sum(projected * projected, axis=1))
        totals = lax.optimization_barrier(jnp.sum(jnp.where(member_m, squares[:, None], 0.0), axis=0))
        image_rms = jnp.sqrt(totals / (areas // 4 * PROJ).astype(jnp.float32))
        sent = send_rows(proj_bf, starts, areas, owner_row, packs)
        return (sent, image_rms, top_logit)
    sent, image_rms, top_logit = lax.map(one_pack, (patches.reshape(packs, TOK_DEV, D), seg_ids.reshape(packs, TOK_DEV), patch_mask.reshape(packs, TOK_DEV), grid_hw.reshape(packs, REQ_DEV, 2), owners.reshape(packs, REQ_DEV)))
    routed = jnp.transpose(sent, (1, 0, 2, 3, 4)).reshape(packs * packs * REQ_DEV * WRAPS, PROJ)
    return (routed, image_rms.reshape(REQS), top_logit.reshape(REQS))
```

```python
import functools
import math

import jax
import jax.numpy as jnp
from jax import lax
from jax.experimental import pallas as pl
from jax.experimental.pallas import tpu as pltpu
from jax.sharding import PartitionSpec as P

HEADS = 8
CAP = 64
LANES = 128
HEAD = 104
QUARTER = 26
ROW = 52
MESH = pl.DeviceIdType.MESH
F32 = jnp.float32
BF16 = jnp.bfloat16


def token_places(seg_row, grid_rows):
    heights = grid_rows[:, 0]
    widths = grid_rows[:, 1]
    areas = heights * widths
    order = jnp.arange(areas.shape[0])
    ends_at = jnp.sum(jnp.where(order[None, :] <= order[:, None], areas[None, :], 0), axis=1)
    starts = ends_at - areas
    image_count = grid_rows.shape[0]
    member = seg_row[:, None] == jnp.arange(image_count, dtype=jnp.int32)[None, :]
    start_tok = jnp.sum(jnp.where(member, starts[None, :], 0), axis=1)
    half_w = jnp.maximum(jnp.sum(jnp.where(member, (widths // 2)[None, :], 0), axis=1), 1)
    offset = jnp.arange(seg_row.shape[0], dtype=jnp.int32) - start_tok
    window = offset // 4
    corner = offset % 4
    row_pos = 2 * (window // half_w) + corner // 2
    col_pos = 2 * (window % half_w) + corner % 2
    return (row_pos.astype(jnp.float32), col_pos.astype(jnp.float32), areas, starts)


def rope_tables(row_pos, col_pos, head_dim):
    quarter = head_dim // 4
    lane = jnp.arange(LANES, dtype=jnp.int32)
    theta = 100.0 ** (-(lane % quarter).astype(jnp.float32) / quarter)
    part = lane // quarter
    pos = jnp.where(part[None, :] < 2, row_pos[:, None], col_pos[:, None])
    angles = pos * theta[None, :]
    cosine = jnp.cos(angles)
    sine = jnp.sin(angles)
    first = (part == 0) | (part == 2)
    second = (part == 1) | (part == 3)
    return (
        cosine,
        jnp.where(first[None, :], -sine, 0.0),
        jnp.where(second[None, :], sine, 0.0),
    )


def send_rows(proj_bf, starts, areas, owner_row, device_count):
    merged_rows = proj_bf.shape[0]
    wrap_count = (CAP + device_count - 1) // device_count
    dest_ids = jnp.arange(device_count, dtype=jnp.int32)[:, None, None]
    wrap_ids = jnp.arange(wrap_count, dtype=jnp.int32)[None, None, :]
    owner_here = owner_row[None, :, None]
    row_within = wrap_ids * device_count + (dest_ids - owner_here) % device_count
    row_total = (areas // 4)[None, :, None]
    first_row = (starts // 4)[None, :, None]
    picked = jnp.where(row_within < row_total, first_row + row_within, merged_rows)
    padded = jnp.concatenate([proj_bf, jnp.zeros((1, proj_bf.shape[1]), proj_bf.dtype)], axis=0)
    return padded[picked]


def plain_gathers(patches, ln_gain, tables, seg_ids, patch_mask, w_qkv, w_out, w_proj):
    tok_count = patches.shape[0]
    tokens_f = patches.astype(jnp.float32)
    mean_row = jnp.mean(tokens_f, axis=-1, keepdims=True)
    centered = tokens_f - mean_row
    var_row = jnp.mean(centered * centered, axis=-1, keepdims=True)
    normed = (centered * lax.rsqrt(var_row + 1e-06) * ln_gain).astype(jnp.bfloat16)
    hidden_w = w_out.shape[0]
    head_dim = hidden_w // HEADS
    quarter = head_dim // 4
    mixed = jnp.dot(
        normed, lax.all_gather(w_qkv, "dp", axis=0, tiled=True), preferred_element_type=jnp.float32
    )
    shape_three = (tok_count, HEADS, head_dim)
    cosine, sin_a, sin_b = [t[:, None, :head_dim] for t in tables]

    def rotate(val):
        return (
            val * cosine
            + jnp.roll(val, -quarter, axis=2) * sin_a
            + jnp.roll(val, quarter, axis=2) * sin_b
        ).astype(jnp.bfloat16)

    queries = rotate(mixed[:, :hidden_w].reshape(shape_three))
    key_rows = rotate(mixed[:, hidden_w : 2 * hidden_w].reshape(shape_three))
    values = mixed[:, 2 * hidden_w :].reshape(shape_three).astype(jnp.bfloat16)
    scores = jnp.einsum("qhd,khd->hqk", queries, key_rows, preferred_element_type=jnp.float32)
    idx = jnp.arange(tok_count, dtype=jnp.int32)
    allowed = (seg_ids[:, None] == seg_ids[None, :]) & (
        (patch_mask[None, :] == 1) | (idx[:, None] == idx[None, :])
    )
    masked = jnp.where(allowed[None], scores * head_dim ** (-0.5), -1e30)
    weights = jax.nn.softmax(masked, axis=-1).astype(jnp.bfloat16)
    attended = jnp.einsum("hqk,khd->qhd", weights, values, preferred_element_type=jnp.float32)
    attended = attended.astype(jnp.bfloat16).reshape(tok_count, hidden_w)
    out_term = jnp.dot(
        attended,
        lax.all_gather(w_out, "dp", axis=1, tiled=True),
        preferred_element_type=jnp.float32,
    )
    return out_term, jnp.max(masked, axis=(0, 2)), lax.all_gather(w_proj, "dp", axis=0, tiled=True)


def any_slice(patches, ln_gain, w_qkv, w_out, w_proj, seg_ids, patch_mask, grid_hw, owners):
    tok_count, width_in = patches.shape
    head_dim = w_out.shape[0] // HEADS
    image_count = grid_hw.shape[0]
    proj_w = w_proj.shape[1]
    devices = lax.axis_size("dp")
    tokens_f = patches.astype(jnp.float32)
    row_pos, col_pos, areas, starts = token_places(seg_ids, grid_hw)
    tables = rope_tables(row_pos, col_pos, head_dim)
    image_ids = jnp.arange(image_count, dtype=jnp.int32)
    out_term, row_top, wp = plain_gathers(
        patches, ln_gain, tables, seg_ids, patch_mask, w_qkv, w_out, w_proj
    )
    member_q = seg_ids[:, None] == image_ids[None, :]
    top_logit = jnp.max(jnp.where(member_q, row_top[:, None], -1e30), axis=0)
    residual = (tokens_f + out_term).astype(jnp.bfloat16)
    merged = residual.reshape(tok_count // 4, 4 * width_in)
    projected = jnp.dot(merged, wp, preferred_element_type=jnp.float32)
    proj_bf = projected.astype(jnp.bfloat16)
    merged_seg = seg_ids.reshape(-1, 4)[:, 0]
    member_m = merged_seg[:, None] == image_ids[None, :]
    squares = jnp.sum(projected * projected, axis=1)
    totals = jnp.sum(jnp.where(member_m, squares[:, None], 0.0), axis=0)
    image_rms = jnp.sqrt(totals / (areas // 4 * proj_w).astype(jnp.float32))
    sent = send_rows(proj_bf, starts, areas, owners, devices)
    arrived = lax.all_to_all(sent, "dp", split_axis=0, concat_axis=0, tiled=True)
    return (arrived.reshape(-1, proj_w), image_rms, top_logit)


class Place:
    def __init__(self):
        me = lax.axis_index("dp")
        self.core = me % 2
        self.x = (me // 2) % 2
        self.y = (me // 4) % 2
        self.z = me // 8
        self.inner = (self.z == 1) | (self.z == 2)

    def line(self, r):
        z = self.z
        return (z, z + 1 - 2 * (z % 2), z + 2 - 4 * (z // 2), 3 - z)[r]

    def device(self, z, y, x, core):
        return ((z * 2 + y) * 2 + x) * 2 + core

    def peer(self, name):
        z, y, x, c = self.z, self.y, self.x, self.core
        if name == "x":
            return self.device(z, y, 1 - x, c)
        if name == "y":
            return self.device(z, 1 - y, x, c)
        if name == "t":
            return self.device(z, y, x, 1 - c)
        return self.device(self.line(int(name[1])), y, x, c)

    def greet(self):
        barrier = pltpu.get_barrier_semaphore()
        peers = [self.peer(n) for n in ("x", "y", "t", "z1", "z2", "z3")]
        for p in peers:
            pl.semaphore_signal(barrier, inc=1, device_id=(p,), device_id_type=MESH)
        pl.semaphore_wait(barrier, len(peers))


class Wires:
    def __init__(self, place, send, recv, local):
        self.place, self.send, self.recv, self.local = place, send, recv, local
        self.used = 0
        self.locals = 0
        self.sent = []

    def copy(self, src, dst, to, only=None, slot=None):
        n = self.used
        self.used += 1
        got = n if slot is None else slot
        c = pltpu.make_async_remote_copy(
            src_ref=src, dst_ref=dst, send_sem=self.send.at[n], recv_sem=self.recv.at[got],
            device_id=(self.place.peer(to),), device_id_type=MESH)
        if only is None:
            c.start()
        else:
            pl.when(only)(c.start)
        self.sent.append((c, only))
        return got, c

    def own(self, src, dst):
        c = pltpu.make_async_copy(src, dst, self.local.at[self.locals])
        self.locals += 1
        c.start()
        return c


class Pairs:
    stages = 6

    def __init__(self, wires, first, src, dst):
        self.w, self.first, self.src, self.dst = wires, first, src, dst
        self.second = "y" if first == "x" else "x"

    def pair(self, r, far):
        p = self.w.place
        z = p.line(r)
        if self.first == "x":
            return self.dst(z, 1 - p.y if far else p.y, None)
        return self.dst(z, None, 1 - p.x if far else p.x)

    def stage(self, n):
        w, p = self.w, self.w.place
        if n == 0:
            mine = self.dst(p.z, p.y, p.x)
            self.mine = w.own(self.src, mine)
            self.from_first = w.copy(self.src, mine, self.first)[1]
        elif n == 1:
            self.mine.wait()
            self.from_first.wait_recv()
            own = self.pair(0, False)
            self.z2 = w.copy(own, own, "z2")
            self.z1 = w.copy(own, own, "z1")
            self.z3 = w.copy(own, own, "z3", only=p.inner)
            self.far = [w.copy(own, own, self.second)[1]]
        elif n == 2:
            self.z2[1].wait_recv()
            got = self.pair(2, False)
            w.copy(got, got, "z1", only=p.inner, slot=self.z3[0])
            self.spread(got)
            self.z1[1].wait_recv()
            self.spread(self.pair(1, False))
        elif n == 3:
            self.z3[1].wait_recv()
            self.spread(self.pair(3, False))
        elif n == 4:
            for copy in self.far:
                copy.wait_recv()
            whole = self.dst(None, None, None)
            self.twin = w.copy(whole, whole, "t")[1]
        elif n == 5:
            self.twin.wait_recv()

    def spread(self, got):
        self.far.append(self.w.copy(got, got, self.second)[1])


class Lines:
    stages = 6

    def __init__(self, wires, src, dst):
        self.w, self.src, self.dst = wires, src, dst

    def column(self, r, s):
        p = self.w.place
        odd = (p.z + r) % 2
        x, y = p.x, p.y
        if s == 0:
            return y, x
        if s == 1:
            return y + odd * (1 - 2 * y), x + (1 - odd) * (1 - 2 * x)
        if s == 2:
            return y + (1 - odd) * (1 - 2 * y), x + odd * (1 - 2 * x)
        return 1 - y, 1 - x

    def unit(self, r, s):
        p = self.w.place
        y, x = self.column(r, s)
        return self.dst(p.line(r), y, x)

    def side(self, r, s):
        p = self.w.place
        y, x = self.column(r, s)
        return p.device(p.z, y, x, p.core)

    def send_side(self, ref, r, s):
        w = self.w
        n = w.used
        w.used += 1
        c = pltpu.make_async_remote_copy(
            src_ref=ref, dst_ref=ref, send_sem=w.send.at[n], recv_sem=w.recv.at[n],
            device_id=(self.side(r, s),), device_id_type=MESH)
        c.start()
        w.sent.append((c, None))
        return c

    def spread(self, r):
        ref = self.unit(r, 0)
        self.s1[r] = self.send_side(ref, r, 1)
        self.s2[r] = self.send_side(ref, r, 2)

    def stage(self, n):
        w, p = self.w, self.w.place
        if n == 0:
            self.s1, self.s2, self.s3 = {}, {}, {}
            mine = self.unit(0, 0)
            self.mine = w.own(self.src, mine)
            self.z2 = w.copy(self.src, mine, "z2")
            self.z1 = w.copy(self.src, mine, "z1")
            self.z3 = w.copy(self.src, mine, "z3", only=p.inner)
        elif n == 1:
            self.mine.wait()
            self.spread(0)
            self.z2[1].wait_recv()
            got = self.unit(2, 0)
            w.copy(got, got, "z1", only=p.inner, slot=self.z3[0])
            self.spread(2)
            self.z1[1].wait_recv()
            self.spread(1)
        elif n == 2:
            self.z3[1].wait_recv()
            self.spread(3)
            for r in (0, 2):
                self.corner(r)
        elif n == 3:
            for r in (1, 3):
                self.corner(r)
        elif n == 4:
            for r in (0, 2, 1, 3):
                self.s2[r].wait_recv()
                self.s3[r].wait_recv()
            whole = self.dst(None, None, None)
            self.twin = w.copy(whole, whole, "t")[1]
        elif n == 5:
            self.twin.wait_recv()

    def corner(self, r):
        self.s1[r].wait_recv()
        ref = self.unit(r, 1)
        self.s3[r] = self.send_side(ref, r, 2)


def finish(wires):
    for c, only in wires.sent:
        if only is None:
            c.wait_send()
        else:
            pl.when(only)(c.wait_send)


class Planes:
    stages = 5

    def __init__(self, wires, src, dst):
        self.w, self.src, self.dst = wires, src, dst

    def unit(self, r):
        return self.dst(self.w.place.line(r), self.w.place.x)

    def spread(self, r):
        ref = self.unit(r)
        self.sides.append(self.w.copy(ref, ref, "x")[1])

    def stage(self, n):
        w, p = self.w, self.w.place
        if n == 0:
            self.sides = []
            mine = self.unit(0)
            self.mine = w.own(self.src, mine)
            self.z2 = w.copy(self.src, mine, "z2")
            self.z1 = w.copy(self.src, mine, "z1")
            self.z3 = w.copy(self.src, mine, "z3", only=p.inner)
        elif n == 1:
            self.mine.wait()
            self.spread(0)
            self.z2[1].wait_recv()
            got = self.unit(2)
            w.copy(got, got, "z1", only=p.inner, slot=self.z3[0])
            self.spread(2)
            self.z1[1].wait_recv()
            self.spread(1)
        elif n == 2:
            self.z3[1].wait_recv()
            self.spread(3)
        elif n == 3:
            for copy in self.sides:
                copy.wait_recv()
            whole = self.dst(None, None)
            self.twin = w.copy(whole, whole, "t")[1]
        elif n == 4:
            self.twin.wait_recv()


class PlanePairs:
    stages = 5

    def __init__(self, wires, src, dst):
        self.w, self.src, self.dst = wires, src, dst

    def stage(self, n):
        w, p = self.w, self.w.place
        if n == 0:
            mine = self.dst(p.z, p.x)
            self.mine = w.own(self.src, mine)
            self.side = w.copy(self.src, mine, "x")[1]
        elif n == 1:
            self.mine.wait()
            self.side.wait_recv()
            pair = self.dst(p.z, None)
            self.z2 = w.copy(pair, pair, "z2")
            self.z1 = w.copy(pair, pair, "z1")
            self.z3 = w.copy(pair, pair, "z3", only=p.inner)
        elif n == 2:
            self.z2[1].wait_recv()
            got = self.dst(p.line(2), None)
            w.copy(got, got, "z1", only=p.inner, slot=self.z3[0])
        elif n == 3:
            self.z1[1].wait_recv()
            self.z3[1].wait_recv()
            whole = self.dst(None, None)
            self.twin = w.copy(whole, whole, "t")[1]
        elif n == 4:
            self.twin.wait_recv()


def image_numbers(grid_ref, owner_ref, j):
    def side(i, k):
        return grid_ref[k : k + 1, i : i + 1]

    start = jnp.zeros((1, 1), jnp.int32)
    for i in range(j):
        start = start + side(i, 0) * side(i, 1)
    return start, side(j, 0) * side(j, 1), side(j, 1), owner_ref[0:1, j : j + 1]


def slot_places(shape, dim, owner, devices):
    slot = lax.broadcasted_iota(jnp.int32, shape, dim)
    corner = slot // CAP
    within = slot % CAP
    row = (within // devices) * devices + (within % devices - owner + devices) % devices
    return row, corner


def whole_kernel(
    devices,
    patches_ref,
    gain_ref,
    wqkv_ref,
    wout_ref,
    mask_ref,
    grid_ref,
    owner_ref,
    wp_ref,
    sent_ref,
    rms_ref,
    top_ref,
    wq_all,
    mine,
    wp_all,
    w_pad,
    quad,
    xs_buf,
    norm_buf,
    qk_buf,
    v_buf,
    cos_buf,
    sin_a_buf,
    sin_b_buf,
    key_buf,
    hall,
    hsend,
    csend,
    crecv,
    cown,
    squares,
    send,
    recv,
    local,
    quad_sem,
):
    place = Place()
    tokens, width = patches_ref.shape
    image = 4 * CAP
    images = tokens // image
    hw = HEADS * HEAD
    scale = HEAD ** (-0.5)

    mine[...] = jnp.zeros_like(mine)
    mine[0:ROW, 0 : 3 * hw] = wqkv_ref[...]
    mine[0:ROW, 3 * hw :] = wout_ref[...]
    place.greet()

    wires = Wires(place, send, recv, local)
    half_cols = mine.shape[1] // 2
    chunks = []
    for n in range(2):
        at = n * half_cols
        pieces = []
        for kind, tiles in (("x", 4), ("y", 4), ("l", 5)):
            cols = slice(at, at + tiles * LANES)
            at += tiles * LANES

            def dst(z, y, x, cols=cols):
                z, y, x = [slice(None) if v is None else v for v in (z, y, x)]
                return wq_all.at[z, y, x, place.core, :, cols]

            src = mine.at[:, cols]
            piece = Lines(wires, src, dst) if kind == "l" else Pairs(wires, kind, src, dst)
            pieces.append(piece)
        chunks.append(pieces)
    p_chunks = csend.shape[0]
    wide = wp_ref.shape[1] // p_chunks
    for n in range(p_chunks):
        cols = slice(n * wide, (n + 1) * wide)

        def dst(z, x, cols=cols):
            z, x = [slice(None) if v is None else v for v in (z, x)]
            return wp_all.at[z, x, place.core, :, cols]

        kind = PlanePairs if n in (4,) else Planes
        chunks.append([kind(wires, wp_ref.at[:, cols], dst)])

    def front(j):
        start, area, w_image, owner = image_numbers(grid_ref, owner_ref, j)
        rows = slice(j * image, (j + 1) * image)
        row, corner = slot_places((image, 1), 0, owner, devices)
        src = jnp.where(row < area // 4, start + 4 * row + corner, -1)
        pick = (lax.broadcasted_iota(jnp.int32, (image, tokens), 1) == src).astype(BF16)
        x = jnp.dot(pick, patches_ref[...], preferred_element_type=F32)
        xs_buf[rows, :] = x.astype(BF16)
        centered = x - jnp.mean(x, axis=1, keepdims=True)
        var = jnp.mean(centered * centered, axis=1, keepdims=True)
        norm_buf[rows, :] = (centered * lax.rsqrt(var + 1e-06) * gain_ref[...][None, :]).astype(BF16)
        keys = lax.dot_general(
            jnp.broadcast_to((mask_ref[...] == 1).astype(F32), (16, tokens)).astype(BF16),
            pick,
            (((1,), (1,)), ((), ())),
            preferred_element_type=F32,
        )
        key_buf[j] = keys[0:8, :]
        half_w = (w_image // 2).astype(F32)
        row_f = row.astype(F32)
        down = jnp.floor((row_f + 0.5) / half_w)
        across = row_f - down * half_w
        bottom = (corner // 2).astype(F32)
        right = (corner % 2).astype(F32)
        row_pos = 2.0 * down + bottom
        col_pos = 2.0 * across + right
        lane = lax.broadcasted_iota(jnp.int32, (1, LANES), 1)
        part = lane // QUARTER
        theta = jnp.exp((lane % QUARTER).astype(F32) * (-math.log(100.0) / QUARTER))
        angles = jnp.where(part < 2, row_pos, col_pos) * theta
        cosine = jnp.cos(angles)
        sine = jnp.sin(angles)
        cos_buf[rows, :] = jnp.where(part < 4, cosine, 0.0)
        sin_a_buf[rows, :] = jnp.where((part == 0) | (part == 2), -sine, 0.0)
        sin_b_buf[rows, :] = jnp.where((part == 1) | (part == 3), sine, 0.0)

    def spread_heads(half):
        cols = slice(half * half_cols, (half + 1) * half_cols)
        count = half_cols // HEAD

        def load(g, slot):
            return pltpu.make_async_copy(
                wq_all.at[g // 2, g % 2, :, :, :, cols], quad.at[slot], quad_sem.at[slot]
            )

        load(0, 0).start()

        def body(g, carry):
            slot = g % 2

            @pl.when(g < 7)
            def _():
                load(g + 1, 1 - slot).start()

            load(g, slot).wait()
            block = jnp.concatenate(
                [quad[slot, i // 2, i % 2, 0:ROW, :].astype(F32) for i in range(4)], axis=0
            )
            rows = pl.ds(pl.multiple_of(g * 4 * ROW, 16), 4 * ROW)
            lane = lax.broadcasted_iota(jnp.int32, (4 * ROW, LANES), 1)
            for h in range(count):
                tile = HEAD * h // LANES * LANES
                off = HEAD * h - tile
                if off + HEAD <= LANES:
                    val = block[:, tile : tile + LANES]
                    if off:
                        val = pltpu.roll(val, LANES - off, 1)
                else:
                    val = pltpu.roll(block[:, tile : tile + 2 * LANES], 2 * LANES - off, 1)
                    val = val[:, :LANES]
                at = (half * count + h) * LANES
                w_pad[rows, at : at + LANES] = jnp.where(lane < HEAD, val, 0.0).astype(BF16)
            return carry

        lax.fori_loop(0, 8, body, 0)

    wide_heads = HEADS * LANES

    def queries_keys(i):
        rows = slice(i * 512, (i + 1) * 512)

        def body(n, carry):
            cols = pl.ds(pl.multiple_of(n * 512, 512), 512)
            mixed = jnp.dot(norm_buf[rows, :], w_pad[:, cols], preferred_element_type=F32)
            cosine, sin_a, sin_b = cos_buf[rows, :], sin_a_buf[rows, :], sin_b_buf[rows, :]
            outs = []
            for h in range(4):
                val = mixed[:, h * LANES : (h + 1) * LANES]
                val = (
                    val * cosine
                    + pltpu.roll(val, LANES - QUARTER, 1) * sin_a
                    + pltpu.roll(val, QUARTER, 1) * sin_b
                )
                outs.append(val.astype(BF16))
            qk_buf[rows, cols] = jnp.concatenate(outs, axis=1)
            return carry

        lax.fori_loop(0, 2 * wide_heads // 512, body, 0)

    def values():
        def body(i, carry):
            rows = pl.ds(pl.multiple_of(i * 512, 512), 512)
            for n in range(wide_heads // 512):
                cols = slice(n * 512, (n + 1) * 512)
                w_cols = slice(2 * wide_heads + n * 512, 2 * wide_heads + (n + 1) * 512)
                mixed = jnp.dot(norm_buf[rows, :], w_pad[:, w_cols], preferred_element_type=F32)
                v_buf[rows, cols] = mixed.astype(BF16)
            return carry

        lax.fori_loop(0, tokens // 512, body, 0)

    exchanged = []

    def attend(j):
        start, area, w_image, owner = image_numbers(grid_ref, owner_ref, j)
        rows = slice(j * image, (j + 1) * image)
        same = lax.broadcasted_iota(jnp.int32, (image, image), 0) == lax.broadcasted_iota(
            jnp.int32, (image, image), 1
        )
        bias = jnp.where((key_buf[j, 0:1, :] > 0.5) | same, 0.0, -1e30)
        best = jnp.full((image, 1), -1e30, F32)
        row, _ = slot_places((image, 1), 0, owner, devices)
        valid = row < area // 4
        for h in range(HEADS):
            lanes = slice(h * LANES, (h + 1) * LANES)
            k_lanes = slice(wide_heads + h * LANES, wide_heads + (h + 1) * LANES)
            scores = lax.dot_general(
                qk_buf[rows, lanes],
                qk_buf[rows, k_lanes],
                (((1,), (1,)), ((), ())),
                preferred_element_type=F32,
            )
            scores = scores * scale + bias
            top = jnp.max(scores, axis=1, keepdims=True)
            best = jnp.maximum(best, top)
            expo = jnp.exp(scores - top)
            total = jnp.sum(expo, axis=1, keepdims=True)
            got = jnp.dot(expo.astype(BF16), v_buf[rows, lanes], preferred_element_type=F32)
            qk_buf[rows, lanes] = (got * jnp.where(valid, 1.0 / total, 0.0)).astype(BF16)
        best = jnp.where(valid, best, -1e30)
        top_ref[j : j + 1, :] = jnp.broadcast_to(
            jnp.max(best, axis=0, keepdims=True), (1, LANES)
        )
        out = lax.dot_general(
            qk_buf[rows, :wide_heads],
            w_pad[:, 3 * wide_heads :],
            (((1,), (1,)), ((), ())),
            preferred_element_type=F32,
        )
        res = out + xs_buf[rows, :].astype(F32)
        turned = pltpu.roll(res, width // 2, 1)
        upper = place.y == 0
        own = jnp.where(upper, res, turned)[:, : width // 2].astype(BF16)
        other = jnp.where(upper, turned, res)[:, : width // 2].astype(BF16)
        at = j * CAP
        for c in range(4):
            hall[c, at : at + CAP, :] = own[c * CAP : (c + 1) * CAP, :]
            hsend[c, at : at + CAP, :] = other[c * CAP : (c + 1) * CAP, :]
        merged_rows = hsend.shape[1]
        exchanged.append(
            wires.copy(
                hsend.at[:, at : at + CAP, :],
                hall.at[:, merged_rows + at : merged_rows + at + CAP, :],
                "y",
            )[1]
        )

    partials = {}

    def project(n):
        if n == 0:
            for c in exchanged:
                c.wait_recv()
        merged_rows = hsend.shape[1]
        cols = slice(n * wide, (n + 1) * wide)
        total = jnp.zeros((2 * merged_rows, wide), F32)
        for c in range(4):
            total = total + jnp.dot(
                hall[c],
                wp_all[c, :, :, :, cols].reshape(width // 2, wide),
                preferred_element_type=F32,
            )
        cown[:, cols] = total[:merged_rows]
        csend[n] = total[merged_rows:].astype(BF16)
        partials[n] = wires.copy(csend.at[n], crecv.at[n], "y")[1]

    def complete(n):
        partials[n].wait_recv()
        merged_rows = hsend.shape[1]
        cols = slice(n * wide, (n + 1) * wide)
        done = cown[:, cols] + crecv[n].astype(F32)
        sq = jnp.sum(done * done, axis=1, keepdims=True)
        if n == 0:
            squares[...] = jnp.broadcast_to(sq, squares.shape)
        else:
            squares[...] += jnp.broadcast_to(sq, squares.shape)
        slots = merged_rows // devices
        out_row = lax.broadcasted_iota(jnp.int32, (merged_rows, merged_rows), 0)
        in_row = lax.broadcasted_iota(jnp.int32, (merged_rows, merged_rows), 1)
        deal = (in_row == (out_row % slots) * devices + out_row // slots).astype(BF16)
        sent_ref[:, cols] = jnp.dot(
            deal, done.astype(BF16), preferred_element_type=F32
        ).astype(BF16)

    work = {
        0: [lambda: front(0)],
        1: [lambda: front(1)],
        2: [lambda: front(2)],
        3: [lambda: front(3)],
        5: [lambda: spread_heads(0), lambda: queries_keys(0), lambda: queries_keys(1)],
        6: [lambda: spread_heads(1), lambda: values(), lambda: attend(0)],
        7: [lambda: attend(1)],
        8: [lambda: attend(2)],
        9: [lambda: attend(3)],
    }
    q_steps = [0, 1, 2, 3, 4, 5]
    p_steps = [0, 2, 2, 5, 6]
    first = 3
    when = [[s + i for s in q_steps] for i in range(2)]
    when += [[s + first + n for s in p_steps] for n in range(p_chunks)]
    for n in range(p_chunks):
        ready = max(10, when[2 + n][-1])
        work.setdefault(ready, []).append(lambda n=n: project(n))
        work.setdefault(ready + 1, []).append(lambda n=n: complete(n))
    for step in range(max(work) + 1):
        for steps, pieces in zip(when, chunks):
            for stage, at in enumerate(steps):
                if at == step:
                    for piece in pieces:
                        piece.stage(stage)
        for task in work.get(step, ()):
            task()
    for j in range(images):
        area = image_numbers(grid_ref, owner_ref, j)[1]
        total = jnp.sum(squares[j * CAP : (j + 1) * CAP, :], axis=0, keepdims=True)
        count = (area // 4 * wp_ref.shape[1]).astype(F32)
        rms_ref[j : j + 1, :] = jnp.sqrt(total / count)
    finish(wires)


def one_kernel(patches, ln_gain, w_qkv, w_out, w_proj, patch_mask, grid_hw, owners, devices):
    tokens, width = patches.shape
    proj_w = w_proj.shape[1]
    merged = tokens // 4
    images = grid_hw.shape[0]
    vmem = pl.BlockSpec(memory_space=pltpu.VMEM)
    hbm = pl.BlockSpec(memory_space=pl.ANY)
    pad_row = 56
    cols = 4 * HEADS * HEAD
    wide = HEADS * LANES
    p_chunks = 8
    scratch = [
        pltpu.VMEM((pad_row, cols), BF16),
        pltpu.VMEM((4, 2, 2) + w_proj.shape, BF16),
        pltpu.VMEM((width, 4 * wide), BF16),
        pltpu.VMEM((2, 2, 2, pad_row, cols // 2), BF16),
        pltpu.VMEM((tokens, width), BF16),
        pltpu.VMEM((tokens, width), BF16),
        pltpu.VMEM((tokens, 2 * wide), BF16),
        pltpu.VMEM((tokens, wide), BF16),
        pltpu.VMEM((tokens, LANES), F32),
        pltpu.VMEM((tokens, LANES), F32),
        pltpu.VMEM((tokens, LANES), F32),
        pltpu.VMEM((images, 8, 4 * CAP), F32),
        pltpu.VMEM((4, 2 * merged, width // 2), BF16),
        pltpu.VMEM((4, merged, width // 2), BF16),
        pltpu.VMEM((p_chunks, merged, proj_w // p_chunks), BF16),
        pltpu.VMEM((p_chunks, merged, proj_w // p_chunks), BF16),
        pltpu.VMEM((merged, proj_w), F32),
        pltpu.VMEM((merged, LANES), F32),
        pltpu.SemaphoreType.DMA((155,)),
        pltpu.SemaphoreType.DMA((155,)),
        pltpu.SemaphoreType.DMA((14,)),
        pltpu.SemaphoreType.DMA((2,)),
    ]
    return pl.pallas_call(
        functools.partial(whole_kernel, devices),
        out_shape=(
            jax.ShapeDtypeStruct((merged, proj_w), BF16),
            jax.ShapeDtypeStruct((8, LANES), F32),
            jax.ShapeDtypeStruct((8, LANES), F32),
            jax.ShapeDtypeStruct((4, 2, 2, 2, pad_row, cols), BF16),
        ),
        in_specs=[vmem] * 7 + [hbm],
        out_specs=(vmem, vmem, vmem, hbm),
        scratch_shapes=scratch,
        compiler_params=pltpu.CompilerParams(
            collective_id=1, has_side_effects=True, vmem_limit_bytes=63 * 1024 * 1024
        ),
    )(
        patches,
        ln_gain,
        w_qkv,
        w_out.T,
        patch_mask[None, :],
        grid_hw.T,
        owners[None, :],
        w_proj,
    )


def this_slice(patches, ln_gain, w_qkv, w_out, w_proj, seg_ids, patch_mask, grid_hw, owners):
    devices = lax.axis_size("dp")
    images = grid_hw.shape[0]
    sent, rms, top, _ = one_kernel(
        patches, ln_gain, w_qkv, w_out, w_proj, patch_mask, grid_hw, owners, devices
    )
    sent = sent.reshape(devices, -1, sent.shape[1])
    arrived = lax.all_to_all(sent, "dp", split_axis=0, concat_axis=0, tiled=True)
    return arrived.reshape(-1, sent.shape[2]), rms[:images, 0], top[:images, 0]


def on_device(*args):
    path = this_slice if lax.axis_size("dp") == 32 else any_slice
    return path(*args)


def solution(mesh):
    return jax.shard_map(
        on_device,
        mesh=mesh,
        in_specs=(
            P("dp", None),
            P(),
            P("dp", None),
            P(None, "dp"),
            P("dp", None),
            P("dp"),
            P("dp"),
            P("dp", None),
            P("dp"),
        ),
        out_specs=(P("dp", None), P("dp"), P("dp")),
        check_vma=False,
    )
```

```python
import functools
import math

import jax
import jax.numpy as jnp
from jax import lax
from jax.experimental import pallas as pl
from jax.experimental.pallas import tpu as pltpu
from jax.sharding import PartitionSpec as P

HEADS = 8
CAP = 64
LANES = 128
HEAD = 104
QUARTER = 26
ROW = 52
MESH = pl.DeviceIdType.MESH
F32 = jnp.float32
BF16 = jnp.bfloat16


def token_places(seg_row, grid_rows):
    heights = grid_rows[:, 0]
    widths = grid_rows[:, 1]
    areas = heights * widths
    order = jnp.arange(areas.shape[0])
    ends_at = jnp.sum(jnp.where(order[None, :] <= order[:, None], areas[None, :], 0), axis=1)
    starts = ends_at - areas
    image_count = grid_rows.shape[0]
    member = seg_row[:, None] == jnp.arange(image_count, dtype=jnp.int32)[None, :]
    start_tok = jnp.sum(jnp.where(member, starts[None, :], 0), axis=1)
    half_w = jnp.maximum(jnp.sum(jnp.where(member, (widths // 2)[None, :], 0), axis=1), 1)
    offset = jnp.arange(seg_row.shape[0], dtype=jnp.int32) - start_tok
    window = offset // 4
    corner = offset % 4
    row_pos = 2 * (window // half_w) + corner // 2
    col_pos = 2 * (window % half_w) + corner % 2
    return (row_pos.astype(jnp.float32), col_pos.astype(jnp.float32), areas, starts)


def rope_tables(row_pos, col_pos, head_dim):
    quarter = head_dim // 4
    lane = jnp.arange(LANES, dtype=jnp.int32)
    theta = 100.0 ** (-(lane % quarter).astype(jnp.float32) / quarter)
    part = lane // quarter
    pos = jnp.where(part[None, :] < 2, row_pos[:, None], col_pos[:, None])
    angles = pos * theta[None, :]
    cosine = jnp.cos(angles)
    sine = jnp.sin(angles)
    first = (part == 0) | (part == 2)
    second = (part == 1) | (part == 3)
    return (
        cosine,
        jnp.where(first[None, :], -sine, 0.0),
        jnp.where(second[None, :], sine, 0.0),
    )


def send_rows(proj_bf, starts, areas, owner_row, device_count):
    merged_rows = proj_bf.shape[0]
    wrap_count = (CAP + device_count - 1) // device_count
    dest_ids = jnp.arange(device_count, dtype=jnp.int32)[:, None, None]
    wrap_ids = jnp.arange(wrap_count, dtype=jnp.int32)[None, None, :]
    owner_here = owner_row[None, :, None]
    row_within = wrap_ids * device_count + (dest_ids - owner_here) % device_count
    row_total = (areas // 4)[None, :, None]
    first_row = (starts // 4)[None, :, None]
    picked = jnp.where(row_within < row_total, first_row + row_within, merged_rows)
    padded = jnp.concatenate([proj_bf, jnp.zeros((1, proj_bf.shape[1]), proj_bf.dtype)], axis=0)
    return padded[picked]


def plain_gathers(patches, ln_gain, tables, seg_ids, patch_mask, w_qkv, w_out, w_proj):
    tok_count = patches.shape[0]
    tokens_f = patches.astype(jnp.float32)
    mean_row = jnp.mean(tokens_f, axis=-1, keepdims=True)
    centered = tokens_f - mean_row
    var_row = jnp.mean(centered * centered, axis=-1, keepdims=True)
    normed = (centered * lax.rsqrt(var_row + 1e-06) * ln_gain).astype(jnp.bfloat16)
    hidden_w = w_out.shape[0]
    head_dim = hidden_w // HEADS
    quarter = head_dim // 4
    mixed = jnp.dot(
        normed, lax.all_gather(w_qkv, "dp", axis=0, tiled=True), preferred_element_type=jnp.float32
    )
    shape_three = (tok_count, HEADS, head_dim)
    cosine, sin_a, sin_b = [t[:, None, :head_dim] for t in tables]

    def rotate(val):
        return (
            val * cosine
            + jnp.roll(val, -quarter, axis=2) * sin_a
            + jnp.roll(val, quarter, axis=2) * sin_b
        ).astype(jnp.bfloat16)

    queries = rotate(mixed[:, :hidden_w].reshape(shape_three))
    key_rows = rotate(mixed[:, hidden_w : 2 * hidden_w].reshape(shape_three))
    values = mixed[:, 2 * hidden_w :].reshape(shape_three).astype(jnp.bfloat16)
    scores = jnp.einsum("qhd,khd->hqk", queries, key_rows, preferred_element_type=jnp.float32)
    idx = jnp.arange(tok_count, dtype=jnp.int32)
    allowed = (seg_ids[:, None] == seg_ids[None, :]) & (
        (patch_mask[None, :] == 1) | (idx[:, None] == idx[None, :])
    )
    masked = jnp.where(allowed[None], scores * head_dim ** (-0.5), -1e30)
    weights = jax.nn.softmax(masked, axis=-1).astype(jnp.bfloat16)
    attended = jnp.einsum("hqk,khd->qhd", weights, values, preferred_element_type=jnp.float32)
    attended = attended.astype(jnp.bfloat16).reshape(tok_count, hidden_w)
    out_term = jnp.dot(
        attended,
        lax.all_gather(w_out, "dp", axis=1, tiled=True),
        preferred_element_type=jnp.float32,
    )
    return out_term, jnp.max(masked, axis=(0, 2)), lax.all_gather(w_proj, "dp", axis=0, tiled=True)


def any_slice(patches, ln_gain, w_qkv, w_out, w_proj, seg_ids, patch_mask, grid_hw, owners):
    tok_count, width_in = patches.shape
    head_dim = w_out.shape[0] // HEADS
    image_count = grid_hw.shape[0]
    proj_w = w_proj.shape[1]
    devices = lax.axis_size("dp")
    tokens_f = patches.astype(jnp.float32)
    row_pos, col_pos, areas, starts = token_places(seg_ids, grid_hw)
    tables = rope_tables(row_pos, col_pos, head_dim)
    image_ids = jnp.arange(image_count, dtype=jnp.int32)
    out_term, row_top, wp = plain_gathers(
        patches, ln_gain, tables, seg_ids, patch_mask, w_qkv, w_out, w_proj
    )
    member_q = seg_ids[:, None] == image_ids[None, :]
    top_logit = jnp.max(jnp.where(member_q, row_top[:, None], -1e30), axis=0)
    residual = (tokens_f + out_term).astype(jnp.bfloat16)
    merged = residual.reshape(tok_count // 4, 4 * width_in)
    projected = jnp.dot(merged, wp, preferred_element_type=jnp.float32)
    proj_bf = projected.astype(jnp.bfloat16)
    merged_seg = seg_ids.reshape(-1, 4)[:, 0]
    member_m = merged_seg[:, None] == image_ids[None, :]
    squares = jnp.sum(projected * projected, axis=1)
    totals = jnp.sum(jnp.where(member_m, squares[:, None], 0.0), axis=0)
    image_rms = jnp.sqrt(totals / (areas // 4 * proj_w).astype(jnp.float32))
    sent = send_rows(proj_bf, starts, areas, owners, devices)
    arrived = lax.all_to_all(sent, "dp", split_axis=0, concat_axis=0, tiled=True)
    return (arrived.reshape(-1, proj_w), image_rms, top_logit)


class Place:
    def __init__(self):
        me = lax.axis_index("dp")
        self.core = me % 2
        self.x = (me // 2) % 2
        self.y = (me // 4) % 2
        self.z = me // 8
        self.inner = (self.z == 1) | (self.z == 2)

    def line(self, r):
        z = self.z
        return (z, z + 1 - 2 * (z % 2), z + 2 - 4 * (z // 2), 3 - z)[r]

    def device(self, z, y, x, core):
        return ((z * 2 + y) * 2 + x) * 2 + core

    def peer(self, name):
        z, y, x, c = self.z, self.y, self.x, self.core
        if name == "x":
            return self.device(z, y, 1 - x, c)
        if name == "y":
            return self.device(z, 1 - y, x, c)
        if name == "t":
            return self.device(z, y, x, 1 - c)
        return self.device(self.line(int(name[1])), y, x, c)

    def greet(self, devices):
        barrier = pltpu.get_barrier_semaphore()
        me = lax.axis_index("dp")

        def hello(k, carry):
            other = lax.rem(me + k, devices)
            pl.semaphore_signal(barrier, inc=1, device_id=(other,), device_id_type=MESH)
            return carry

        lax.fori_loop(1, devices, hello, 0)
        pl.semaphore_wait(barrier, devices - 1)


class Wires:
    def __init__(self, place, send, recv, local):
        self.place, self.send, self.recv, self.local = place, send, recv, local
        self.used = 0
        self.locals = 0
        self.sent = []

    def copy(self, src, dst, to, only=None, slot=None):
        n = self.used
        self.used += 1
        got = n if slot is None else slot
        c = pltpu.make_async_remote_copy(
            src_ref=src, dst_ref=dst, send_sem=self.send.at[n], recv_sem=self.recv.at[got],
            device_id=(self.place.peer(to),), device_id_type=MESH)
        if only is None:
            c.start()
        else:
            pl.when(only)(c.start)
        self.sent.append((c, only))
        return got, c

    def own(self, src, dst):
        c = pltpu.make_async_copy(src, dst, self.local.at[self.locals])
        self.locals += 1
        c.start()
        return c


class Pairs:
    stages = 6

    def __init__(self, wires, first, src, dst):
        self.w, self.first, self.src, self.dst = wires, first, src, dst
        self.second = "y" if first == "x" else "x"

    def pair(self, r, far):
        p = self.w.place
        z = p.line(r)
        if self.first == "x":
            return self.dst(z, 1 - p.y if far else p.y, None)
        return self.dst(z, None, 1 - p.x if far else p.x)

    def stage(self, n):
        w, p = self.w, self.w.place
        if n == 0:
            mine = self.dst(p.z, p.y, p.x)
            self.mine = w.own(self.src, mine)
            self.from_first = w.copy(self.src, mine, self.first)[1]
        elif n == 1:
            self.mine.wait()
            self.from_first.wait_recv()
            own = self.pair(0, False)
            self.z2 = w.copy(own, own, "z2")
            self.z1 = w.copy(own, own, "z1")
            self.z3 = w.copy(own, own, "z3", only=p.inner)
            self.far = [w.copy(own, own, self.second)[1]]
        elif n == 2:
            self.z2[1].wait_recv()
            got = self.pair(2, False)
            w.copy(got, got, "z1", only=p.inner, slot=self.z3[0])
            self.spread(got)
            self.z1[1].wait_recv()
            self.spread(self.pair(1, False))
        elif n == 3:
            self.z3[1].wait_recv()
            self.spread(self.pair(3, False))
        elif n == 4:
            for copy in self.far:
                copy.wait_recv()
            whole = self.dst(None, None, None)
            self.twin = w.copy(whole, whole, "t")[1]
        elif n == 5:
            self.twin.wait_recv()

    def spread(self, got):
        self.far.append(self.w.copy(got, got, self.second)[1])


class Lines:
    stages = 6

    def __init__(self, wires, src, dst):
        self.w, self.src, self.dst = wires, src, dst

    def column(self, r, s):
        p = self.w.place
        odd = (p.z + r) % 2
        x, y = p.x, p.y
        if s == 0:
            return y, x
        if s == 1:
            return y + odd * (1 - 2 * y), x + (1 - odd) * (1 - 2 * x)
        if s == 2:
            return y + (1 - odd) * (1 - 2 * y), x + odd * (1 - 2 * x)
        return 1 - y, 1 - x

    def unit(self, r, s):
        p = self.w.place
        y, x = self.column(r, s)
        return self.dst(p.line(r), y, x)

    def side(self, r, s):
        p = self.w.place
        y, x = self.column(r, s)
        return p.device(p.z, y, x, p.core)

    def send_side(self, ref, r, s):
        w = self.w
        n = w.used
        w.used += 1
        c = pltpu.make_async_remote_copy(
            src_ref=ref, dst_ref=ref, send_sem=w.send.at[n], recv_sem=w.recv.at[n],
            device_id=(self.side(r, s),), device_id_type=MESH)
        c.start()
        w.sent.append((c, None))
        return c

    def spread(self, r):
        ref = self.unit(r, 0)
        self.s1[r] = self.send_side(ref, r, 1)
        self.s2[r] = self.send_side(ref, r, 2)

    def stage(self, n):
        w, p = self.w, self.w.place
        if n == 0:
            self.s1, self.s2, self.s3 = {}, {}, {}
            mine = self.unit(0, 0)
            self.mine = w.own(self.src, mine)
            self.z2 = w.copy(self.src, mine, "z2")
            self.z1 = w.copy(self.src, mine, "z1")
            self.z3 = w.copy(self.src, mine, "z3", only=p.inner)
        elif n == 1:
            self.mine.wait()
            self.spread(0)
            self.z2[1].wait_recv()
            got = self.unit(2, 0)
            w.copy(got, got, "z1", only=p.inner, slot=self.z3[0])
            self.spread(2)
            self.z1[1].wait_recv()
            self.spread(1)
        elif n == 2:
            self.z3[1].wait_recv()
            self.spread(3)
            for r in (0, 2):
                self.corner(r)
        elif n == 3:
            for r in (1, 3):
                self.corner(r)
        elif n == 4:
            for r in (0, 2, 1, 3):
                self.s2[r].wait_recv()
                self.s3[r].wait_recv()
            whole = self.dst(None, None, None)
            self.twin = w.copy(whole, whole, "t")[1]
        elif n == 5:
            self.twin.wait_recv()

    def corner(self, r):
        self.s1[r].wait_recv()
        ref = self.unit(r, 1)
        self.s3[r] = self.send_side(ref, r, 2)


def finish(wires):
    for c, only in wires.sent:
        if only is None:
            c.wait_send()
        else:
            pl.when(only)(c.wait_send)


class Planes:
    stages = 5

    def __init__(self, wires, src, dst):
        self.w, self.src, self.dst = wires, src, dst

    def unit(self, r):
        return self.dst(self.w.place.line(r), self.w.place.x)

    def spread(self, r):
        ref = self.unit(r)
        self.sides.append(self.w.copy(ref, ref, "x")[1])

    def stage(self, n):
        w, p = self.w, self.w.place
        if n == 0:
            self.sides = []
            mine = self.unit(0)
            self.mine = w.own(self.src, mine)
            self.z2 = w.copy(self.src, mine, "z2")
            self.z1 = w.copy(self.src, mine, "z1")
            self.z3 = w.copy(self.src, mine, "z3", only=p.inner)
        elif n == 1:
            self.mine.wait()
            self.spread(0)
            self.z2[1].wait_recv()
            got = self.unit(2)
            w.copy(got, got, "z1", only=p.inner, slot=self.z3[0])
            self.spread(2)
            self.z1[1].wait_recv()
            self.spread(1)
        elif n == 2:
            self.z3[1].wait_recv()
            self.spread(3)
        elif n == 3:
            for copy in self.sides:
                copy.wait_recv()
            whole = self.dst(None, None)
            self.twin = w.copy(whole, whole, "t")[1]
        elif n == 4:
            self.twin.wait_recv()


class PlanePairs:
    stages = 5

    def __init__(self, wires, src, dst):
        self.w, self.src, self.dst = wires, src, dst

    def stage(self, n):
        w, p = self.w, self.w.place
        if n == 0:
            mine = self.dst(p.z, p.x)
            self.mine = w.own(self.src, mine)
            self.side = w.copy(self.src, mine, "x")[1]
        elif n == 1:
            self.mine.wait()
            self.side.wait_recv()
            pair = self.dst(p.z, None)
            self.z2 = w.copy(pair, pair, "z2")
            self.z1 = w.copy(pair, pair, "z1")
            self.z3 = w.copy(pair, pair, "z3", only=p.inner)
        elif n == 2:
            self.z2[1].wait_recv()
            got = self.dst(p.line(2), None)
            w.copy(got, got, "z1", only=p.inner, slot=self.z3[0])
        elif n == 3:
            self.z1[1].wait_recv()
            self.z3[1].wait_recv()
            whole = self.dst(None, None)
            self.twin = w.copy(whole, whole, "t")[1]
        elif n == 4:
            self.twin.wait_recv()


def image_numbers(grid_ref, owner_ref, j):
    def side(i, k):
        return grid_ref[k : k + 1, i : i + 1]

    start = jnp.zeros((1, 1), jnp.int32)
    for i in range(j):
        start = start + side(i, 0) * side(i, 1)
    return start, side(j, 0) * side(j, 1), side(j, 1), owner_ref[0:1, j : j + 1]


def slot_places(shape, dim, owner, devices):
    slot = lax.broadcasted_iota(jnp.int32, shape, dim)
    corner = slot // CAP
    within = slot % CAP
    row = (within // devices) * devices + (within % devices - owner + devices) % devices
    return row, corner


def whole_kernel(
    devices,
    patches_ref,
    gain_ref,
    wqkv_ref,
    wout_ref,
    mask_ref,
    grid_ref,
    owner_ref,
    wp_ref,
    routed_ref,
    rms_ref,
    top_ref,
    wq_all,
    mine,
    wp_all,
    w_pad,
    quad,
    xs_buf,
    norm_buf,
    qk_buf,
    v_buf,
    cos_buf,
    sin_a_buf,
    sin_b_buf,
    key_buf,
    hall,
    hsend,
    csend,
    crecv,
    cown,
    squares,
    dealt,
    send,
    recv,
    local,
    quad_sem,
    deal_send,
    deal_recv,
    deal_own,
):
    place = Place()
    tokens, width = patches_ref.shape
    image = 4 * CAP
    images = tokens // image
    hw = HEADS * HEAD
    scale = HEAD ** (-0.5)

    mine[...] = jnp.zeros_like(mine)
    mine[0:ROW, 0 : 3 * hw] = wqkv_ref[...]
    mine[0:ROW, 3 * hw :] = wout_ref[...]
    place.greet(devices)

    wires = Wires(place, send, recv, local)
    half_cols = mine.shape[1] // 2
    chunks = []
    for n in range(2):
        at = n * half_cols
        pieces = []
        for kind, tiles in (("x", 4), ("y", 4), ("l", 5)):
            cols = slice(at, at + tiles * LANES)
            at += tiles * LANES

            def dst(z, y, x, cols=cols):
                z, y, x = [slice(None) if v is None else v for v in (z, y, x)]
                return wq_all.at[z, y, x, place.core, :, cols]

            src = mine.at[:, cols]
            piece = Lines(wires, src, dst) if kind == "l" else Pairs(wires, kind, src, dst)
            pieces.append(piece)
        chunks.append(pieces)
    p_chunks = csend.shape[0]
    wide = wp_ref.shape[1] // p_chunks
    for n in range(p_chunks):
        cols = slice(n * wide, (n + 1) * wide)

        def dst(z, x, cols=cols):
            z, x = [slice(None) if v is None else v for v in (z, x)]
            return wp_all.at[z, x, place.core, :, cols]

        kind = PlanePairs if n in (4,) else Planes
        chunks.append([kind(wires, wp_ref.at[:, cols], dst)])

    def front(j):
        start, area, w_image, owner = image_numbers(grid_ref, owner_ref, j)
        rows = slice(j * image, (j + 1) * image)
        row, corner = slot_places((image, 1), 0, owner, devices)
        src = jnp.where(row < area // 4, start + 4 * row + corner, -1)
        pick = (lax.broadcasted_iota(jnp.int32, (image, tokens), 1) == src).astype(BF16)
        x = jnp.dot(pick, patches_ref[...], preferred_element_type=F32)
        xs_buf[rows, :] = x.astype(BF16)
        centered = x - jnp.mean(x, axis=1, keepdims=True)
        var = jnp.mean(centered * centered, axis=1, keepdims=True)
        norm_buf[rows, :] = (centered * lax.rsqrt(var + 1e-06) * gain_ref[...][None, :]).astype(BF16)
        keys = lax.dot_general(
            jnp.broadcast_to((mask_ref[...] == 1).astype(F32), (16, tokens)).astype(BF16),
            pick,
            (((1,), (1,)), ((), ())),
            preferred_element_type=F32,
        )
        key_buf[j] = keys[0:8, :]
        half_w = (w_image // 2).astype(F32)
        row_f = row.astype(F32)
        down = jnp.floor((row_f + 0.5) / half_w)
        across = row_f - down * half_w
        bottom = (corner // 2).astype(F32)
        right = (corner % 2).astype(F32)
        row_pos = 2.0 * down + bottom
        col_pos = 2.0 * across + right
        lane = lax.broadcasted_iota(jnp.int32, (1, LANES), 1)
        part = lane // QUARTER
        theta = jnp.exp((lane % QUARTER).astype(F32) * (-math.log(100.0) / QUARTER))
        angles = jnp.where(part < 2, row_pos, col_pos) * theta
        cosine = jnp.cos(angles)
        sine = jnp.sin(angles)
        cos_buf[rows, :] = jnp.where(part < 4, cosine, 0.0)
        sin_a_buf[rows, :] = jnp.where((part == 0) | (part == 2), -sine, 0.0)
        sin_b_buf[rows, :] = jnp.where((part == 1) | (part == 3), sine, 0.0)

    def spread_heads(half):
        cols = slice(half * half_cols, (half + 1) * half_cols)
        count = half_cols // HEAD

        def load(g, slot):
            return pltpu.make_async_copy(
                wq_all.at[g // 2, g % 2, :, :, :, cols], quad.at[slot], quad_sem.at[slot]
            )

        load(0, 0).start()

        def body(g, carry):
            slot = g % 2

            @pl.when(g < 7)
            def _():
                load(g + 1, 1 - slot).start()

            load(g, slot).wait()
            block = jnp.concatenate(
                [quad[slot, i // 2, i % 2, 0:ROW, :].astype(F32) for i in range(4)], axis=0
            )
            rows = pl.ds(pl.multiple_of(g * 4 * ROW, 16), 4 * ROW)
            lane = lax.broadcasted_iota(jnp.int32, (4 * ROW, LANES), 1)
            for h in range(count):
                tile = HEAD * h // LANES * LANES
                off = HEAD * h - tile
                if off + HEAD <= LANES:
                    val = block[:, tile : tile + LANES]
                    if off:
                        val = pltpu.roll(val, LANES - off, 1)
                else:
                    val = pltpu.roll(block[:, tile : tile + 2 * LANES], 2 * LANES - off, 1)
                    val = val[:, :LANES]
                at = (half * count + h) * LANES
                w_pad[rows, at : at + LANES] = jnp.where(lane < HEAD, val, 0.0).astype(BF16)
            return carry

        lax.fori_loop(0, 8, body, 0)

    wide_heads = HEADS * LANES

    def queries_keys(i):
        rows = slice(i * 512, (i + 1) * 512)

        def body(n, carry):
            cols = pl.ds(pl.multiple_of(n * 512, 512), 512)
            mixed = jnp.dot(norm_buf[rows, :], w_pad[:, cols], preferred_element_type=F32)
            cosine, sin_a, sin_b = cos_buf[rows, :], sin_a_buf[rows, :], sin_b_buf[rows, :]
            outs = []
            for h in range(4):
                val = mixed[:, h * LANES : (h + 1) * LANES]
                val = (
                    val * cosine
                    + pltpu.roll(val, LANES - QUARTER, 1) * sin_a
                    + pltpu.roll(val, QUARTER, 1) * sin_b
                )
                outs.append(val.astype(BF16))
            qk_buf[rows, cols] = jnp.concatenate(outs, axis=1)
            return carry

        lax.fori_loop(0, 2 * wide_heads // 512, body, 0)

    def values():
        def body(i, carry):
            rows = pl.ds(pl.multiple_of(i * 512, 512), 512)
            for n in range(wide_heads // 512):
                cols = slice(n * 512, (n + 1) * 512)
                w_cols = slice(2 * wide_heads + n * 512, 2 * wide_heads + (n + 1) * 512)
                mixed = jnp.dot(norm_buf[rows, :], w_pad[:, w_cols], preferred_element_type=F32)
                v_buf[rows, cols] = mixed.astype(BF16)
            return carry

        lax.fori_loop(0, tokens // 512, body, 0)

    exchanged = []

    def attend(j):
        start, area, w_image, owner = image_numbers(grid_ref, owner_ref, j)
        rows = slice(j * image, (j + 1) * image)
        same = lax.broadcasted_iota(jnp.int32, (image, image), 0) == lax.broadcasted_iota(
            jnp.int32, (image, image), 1
        )
        bias = jnp.where((key_buf[j, 0:1, :] > 0.5) | same, 0.0, -1e30)
        best = jnp.full((image, 1), -1e30, F32)
        row, _ = slot_places((image, 1), 0, owner, devices)
        valid = row < area // 4
        for h in range(HEADS):
            lanes = slice(h * LANES, (h + 1) * LANES)
            k_lanes = slice(wide_heads + h * LANES, wide_heads + (h + 1) * LANES)
            scores = lax.dot_general(
                qk_buf[rows, lanes],
                qk_buf[rows, k_lanes],
                (((1,), (1,)), ((), ())),
                preferred_element_type=F32,
            )
            scores = scores * scale + bias
            top = jnp.max(scores, axis=1, keepdims=True)
            best = jnp.maximum(best, top)
            expo = jnp.exp(scores - top)
            total = jnp.sum(expo, axis=1, keepdims=True)
            got = jnp.dot(expo.astype(BF16), v_buf[rows, lanes], preferred_element_type=F32)
            qk_buf[rows, lanes] = (got * jnp.where(valid, 1.0 / total, 0.0)).astype(BF16)
        best = jnp.where(valid, best, -1e30)
        top_ref[j : j + 1, :] = jnp.broadcast_to(
            jnp.max(best, axis=0, keepdims=True), (1, LANES)
        )
        out = lax.dot_general(
            qk_buf[rows, :wide_heads],
            w_pad[:, 3 * wide_heads :],
            (((1,), (1,)), ((), ())),
            preferred_element_type=F32,
        )
        res = out + xs_buf[rows, :].astype(F32)
        turned = pltpu.roll(res, width // 2, 1)
        upper = place.y == 0
        own = jnp.where(upper, res, turned)[:, : width // 2].astype(BF16)
        other = jnp.where(upper, turned, res)[:, : width // 2].astype(BF16)
        at = j * CAP
        for c in range(4):
            hall[c, at : at + CAP, :] = own[c * CAP : (c + 1) * CAP, :]
            hsend[c, at : at + CAP, :] = other[c * CAP : (c + 1) * CAP, :]
        merged_rows = hsend.shape[1]
        exchanged.append(
            wires.copy(
                hsend.at[:, at : at + CAP, :],
                hall.at[:, merged_rows + at : merged_rows + at + CAP, :],
                "y",
            )[1]
        )

    partials = {}

    def project(n):
        if n == 0:
            for c in exchanged:
                c.wait_recv()
        merged_rows = hsend.shape[1]
        cols = slice(n * wide, (n + 1) * wide)
        total = jnp.zeros((2 * merged_rows, wide), F32)
        for c in range(4):
            total = total + jnp.dot(
                hall[c],
                wp_all[c, :, :, :, cols].reshape(width // 2, wide),
                preferred_element_type=F32,
            )
        cown[:, cols] = total[:merged_rows]
        csend[n] = total[merged_rows:].astype(BF16)
        partials[n] = wires.copy(csend.at[n], crecv.at[n], "y")[1]

    def complete(n):
        partials[n].wait_recv()
        merged_rows = hsend.shape[1]
        cols = slice(n * wide, (n + 1) * wide)
        done = cown[:, cols] + crecv[n].astype(F32)
        sq = jnp.sum(done * done, axis=1, keepdims=True)
        if n == 0:
            squares[...] = jnp.broadcast_to(sq, squares.shape)
        else:
            squares[...] += jnp.broadcast_to(sq, squares.shape)
        slots = merged_rows // devices
        out_row = lax.broadcasted_iota(jnp.int32, (merged_rows, merged_rows), 0)
        in_row = lax.broadcasted_iota(jnp.int32, (merged_rows, merged_rows), 1)
        deal = (in_row == (out_row % slots) * devices + out_row // slots).astype(BF16)
        out = jnp.dot(deal, done.astype(BF16), preferred_element_type=F32)
        dealt[:, :, cols] = out.reshape(devices, slots, wide).astype(BF16)

    me = lax.axis_index("dp")
    groups = deal_own.shape[0]
    group_cols = wp_ref.shape[1] // groups

    def deal_out(n):
        cols = slice(n * group_cols, (n + 1) * group_cols)
        pltpu.make_async_copy(
            dealt.at[me, :, cols], routed_ref.at[me, :, cols], deal_own.at[n]
        ).start()

        def give(k, carry):
            to = lax.rem(me + k, devices)
            pltpu.make_async_remote_copy(
                src_ref=dealt.at[to, :, cols],
                dst_ref=routed_ref.at[me, :, cols],
                send_sem=deal_send.at[n],
                recv_sem=deal_recv.at[n],
                device_id=(to,),
                device_id_type=MESH,
            ).start()
            return carry

        lax.fori_loop(1, devices, give, 0)

    def dealt_all():
        for n in range(groups):
            cols = slice(n * group_cols, (n + 1) * group_cols)
            others = routed_ref.at[pl.ds(0, devices - 1), :, cols]
            pltpu.make_async_copy(others, others, deal_recv.at[n]).wait()
            given = dealt.at[pl.ds(0, devices - 1), :, cols]
            pltpu.make_async_copy(given, given, deal_send.at[n]).wait()
            pltpu.make_async_copy(
                dealt.at[me, :, cols], routed_ref.at[me, :, cols], deal_own.at[n]
            ).wait()

    work = {
        0: [lambda: front(0)],
        1: [lambda: front(1)],
        2: [lambda: front(2)],
        3: [lambda: front(3)],
        5: [lambda: spread_heads(0)],
        6: [lambda: queries_keys(0)],
        7: [lambda: queries_keys(1)],
        8: [lambda: spread_heads(1)],
        9: [lambda: values(), lambda: attend(0)],
        10: [lambda: attend(1)],
        11: [lambda: attend(2)],
        12: [lambda: attend(3)],
        15: [lambda: project(0), lambda: project(1), lambda: project(2)],
        16: [lambda: project(3), lambda: complete(0), lambda: complete(1)],
        17: [lambda: project(4), lambda: deal_out(0), lambda: complete(2), lambda: complete(3)],
        18: [lambda: project(5), lambda: deal_out(1), lambda: complete(4)],
        19: [lambda: project(6), lambda: complete(5), lambda: deal_out(2)],
        20: [lambda: project(7), lambda: complete(6), lambda: complete(7), lambda: deal_out(3)],
    }
    when = [
        [0, 1, 2, 3, 4, 5],
        [1, 2, 3, 4, 5, 6],
        [3, 5, 6, 9, 10],
        [5, 7, 8, 11, 12],
        [7, 9, 10, 13, 14],
        [9, 11, 12, 14, 15],
        [10, 11, 13, 15, 16],
        [11, 13, 14, 16, 17],
        [12, 14, 15, 17, 18],
        [13, 15, 16, 18, 19],
    ]
    for step in range(max(work) + 1):
        for steps, pieces in zip(when, chunks):
            for stage, at in enumerate(steps):
                if at == step:
                    for piece in pieces:
                        piece.stage(stage)
        for task in work.get(step, ()):
            task()
    for j in range(images):
        area = image_numbers(grid_ref, owner_ref, j)[1]
        total = jnp.sum(squares[j * CAP : (j + 1) * CAP, :], axis=0, keepdims=True)
        count = (area // 4 * wp_ref.shape[1]).astype(F32)
        rms_ref[j : j + 1, :] = jnp.sqrt(total / count)
    finish(wires)
    dealt_all()


def one_kernel(patches, ln_gain, w_qkv, w_out, w_proj, patch_mask, grid_hw, owners, devices):
    tokens, width = patches.shape
    proj_w = w_proj.shape[1]
    merged = tokens // 4
    images = grid_hw.shape[0]
    vmem = pl.BlockSpec(memory_space=pltpu.VMEM)
    hbm = pl.BlockSpec(memory_space=pl.ANY)
    pad_row = 56
    cols = 4 * HEADS * HEAD
    wide = HEADS * LANES
    p_chunks = 8
    scratch = [
        pltpu.VMEM((pad_row, cols), BF16),
        pltpu.VMEM((4, 2, 2) + w_proj.shape, BF16),
        pltpu.VMEM((width, 4 * wide), BF16),
        pltpu.VMEM((2, 2, 2, pad_row, cols // 2), BF16),
        pltpu.VMEM((tokens, width), BF16),
        pltpu.VMEM((tokens, width), BF16),
        pltpu.VMEM((tokens, 2 * wide), BF16),
        pltpu.VMEM((tokens, wide), BF16),
        pltpu.VMEM((tokens, LANES), F32),
        pltpu.VMEM((tokens, LANES), F32),
        pltpu.VMEM((tokens, LANES), F32),
        pltpu.VMEM((images, 8, 4 * CAP), F32),
        pltpu.VMEM((4, 2 * merged, width // 2), BF16),
        pltpu.VMEM((4, merged, width // 2), BF16),
        pltpu.VMEM((p_chunks, merged, proj_w // p_chunks), BF16),
        pltpu.VMEM((p_chunks, merged, proj_w // p_chunks), BF16),
        pltpu.VMEM((merged, proj_w), F32),
        pltpu.VMEM((merged, LANES), F32),
        pltpu.VMEM((devices, merged // devices, proj_w), BF16),
        pltpu.SemaphoreType.DMA((155,)),
        pltpu.SemaphoreType.DMA((155,)),
        pltpu.SemaphoreType.DMA((14,)),
        pltpu.SemaphoreType.DMA((2,)),
        pltpu.SemaphoreType.DMA((4,)),
        pltpu.SemaphoreType.DMA((4,)),
        pltpu.SemaphoreType.DMA((4,)),
    ]
    return pl.pallas_call(
        functools.partial(whole_kernel, devices),
        out_shape=(
            jax.ShapeDtypeStruct((devices, merged // devices, proj_w), BF16),
            jax.ShapeDtypeStruct((8, LANES), F32),
            jax.ShapeDtypeStruct((8, LANES), F32),
            jax.ShapeDtypeStruct((4, 2, 2, 2, pad_row, cols), BF16),
        ),
        in_specs=[vmem] * 7 + [hbm],
        out_specs=(hbm, vmem, vmem, hbm),
        scratch_shapes=scratch,
        compiler_params=pltpu.CompilerParams(
            collective_id=1, has_side_effects=True, vmem_limit_bytes=63 * 1024 * 1024
        ),
    )(
        patches,
        ln_gain,
        w_qkv,
        w_out.T,
        patch_mask[None, :],
        grid_hw.T,
        owners[None, :],
        w_proj,
    )


def this_slice(patches, ln_gain, w_qkv, w_out, w_proj, seg_ids, patch_mask, grid_hw, owners):
    devices = lax.axis_size("dp")
    images = grid_hw.shape[0]
    routed, rms, top, _ = one_kernel(
        patches, ln_gain, w_qkv, w_out, w_proj, patch_mask, grid_hw, owners, devices
    )
    return routed.reshape(-1, w_proj.shape[1]), rms[:images, 0], top[:images, 0]


def on_device(*args):
    path = this_slice if lax.axis_size("dp") == 32 else any_slice
    return path(*args)


def solution(mesh):
    return jax.shard_map(
        on_device,
        mesh=mesh,
        in_specs=(
            P("dp", None),
            P(),
            P("dp", None),
            P(None, "dp"),
            P("dp", None),
            P("dp"),
            P("dp"),
            P("dp", None),
            P("dp"),
        ),
        out_specs=(P("dp", None), P("dp"), P("dp")),
        check_vma=False,
    )
```

```python
import functools
import math

import jax
import jax.numpy as jnp
from jax import lax
from jax.experimental import pallas as pl
from jax.experimental.pallas import tpu as pltpu
from jax.sharding import PartitionSpec as P

HEADS = 8
CAP = 64
LANES = 128
HEAD = 104
QUARTER = 26
ROW = 52
MESH = pl.DeviceIdType.MESH
F32 = jnp.float32
BF16 = jnp.bfloat16


def token_places(seg_row, grid_rows):
    heights = grid_rows[:, 0]
    widths = grid_rows[:, 1]
    areas = heights * widths
    order = jnp.arange(areas.shape[0])
    ends_at = jnp.sum(jnp.where(order[None, :] <= order[:, None], areas[None, :], 0), axis=1)
    starts = ends_at - areas
    image_count = grid_rows.shape[0]
    member = seg_row[:, None] == jnp.arange(image_count, dtype=jnp.int32)[None, :]
    start_tok = jnp.sum(jnp.where(member, starts[None, :], 0), axis=1)
    half_w = jnp.maximum(jnp.sum(jnp.where(member, (widths // 2)[None, :], 0), axis=1), 1)
    offset = jnp.arange(seg_row.shape[0], dtype=jnp.int32) - start_tok
    window = offset // 4
    corner = offset % 4
    row_pos = 2 * (window // half_w) + corner // 2
    col_pos = 2 * (window % half_w) + corner % 2
    return (row_pos.astype(jnp.float32), col_pos.astype(jnp.float32), areas, starts)


def rope_tables(row_pos, col_pos, head_dim):
    quarter = head_dim // 4
    lane = jnp.arange(LANES, dtype=jnp.int32)
    theta = 100.0 ** (-(lane % quarter).astype(jnp.float32) / quarter)
    part = lane // quarter
    pos = jnp.where(part[None, :] < 2, row_pos[:, None], col_pos[:, None])
    angles = pos * theta[None, :]
    cosine = jnp.cos(angles)
    sine = jnp.sin(angles)
    first = (part == 0) | (part == 2)
    second = (part == 1) | (part == 3)
    return (
        cosine,
        jnp.where(first[None, :], -sine, 0.0),
        jnp.where(second[None, :], sine, 0.0),
    )


def send_rows(proj_bf, starts, areas, owner_row, device_count):
    merged_rows = proj_bf.shape[0]
    wrap_count = (CAP + device_count - 1) // device_count
    dest_ids = jnp.arange(device_count, dtype=jnp.int32)[:, None, None]
    wrap_ids = jnp.arange(wrap_count, dtype=jnp.int32)[None, None, :]
    owner_here = owner_row[None, :, None]
    row_within = wrap_ids * device_count + (dest_ids - owner_here) % device_count
    row_total = (areas // 4)[None, :, None]
    first_row = (starts // 4)[None, :, None]
    picked = jnp.where(row_within < row_total, first_row + row_within, merged_rows)
    padded = jnp.concatenate([proj_bf, jnp.zeros((1, proj_bf.shape[1]), proj_bf.dtype)], axis=0)
    return padded[picked]


def plain_gathers(patches, ln_gain, tables, seg_ids, patch_mask, w_qkv, w_out, w_proj):
    tok_count = patches.shape[0]
    tokens_f = patches.astype(jnp.float32)
    mean_row = jnp.mean(tokens_f, axis=-1, keepdims=True)
    centered = tokens_f - mean_row
    var_row = jnp.mean(centered * centered, axis=-1, keepdims=True)
    normed = (centered * lax.rsqrt(var_row + 1e-06) * ln_gain).astype(jnp.bfloat16)
    hidden_w = w_out.shape[0]
    head_dim = hidden_w // HEADS
    quarter = head_dim // 4
    mixed = jnp.dot(
        normed, lax.all_gather(w_qkv, "dp", axis=0, tiled=True), preferred_element_type=jnp.float32
    )
    shape_three = (tok_count, HEADS, head_dim)
    cosine, sin_a, sin_b = [t[:, None, :head_dim] for t in tables]

    def rotate(val):
        return (
            val * cosine
            + jnp.roll(val, -quarter, axis=2) * sin_a
            + jnp.roll(val, quarter, axis=2) * sin_b
        ).astype(jnp.bfloat16)

    queries = rotate(mixed[:, :hidden_w].reshape(shape_three))
    key_rows = rotate(mixed[:, hidden_w : 2 * hidden_w].reshape(shape_three))
    values = mixed[:, 2 * hidden_w :].reshape(shape_three).astype(jnp.bfloat16)
    scores = jnp.einsum("qhd,khd->hqk", queries, key_rows, preferred_element_type=jnp.float32)
    idx = jnp.arange(tok_count, dtype=jnp.int32)
    allowed = (seg_ids[:, None] == seg_ids[None, :]) & (
        (patch_mask[None, :] == 1) | (idx[:, None] == idx[None, :])
    )
    masked = jnp.where(allowed[None], scores * head_dim ** (-0.5), -1e30)
    weights = jax.nn.softmax(masked, axis=-1).astype(jnp.bfloat16)
    attended = jnp.einsum("hqk,khd->qhd", weights, values, preferred_element_type=jnp.float32)
    attended = attended.astype(jnp.bfloat16).reshape(tok_count, hidden_w)
    out_term = jnp.dot(
        attended,
        lax.all_gather(w_out, "dp", axis=1, tiled=True),
        preferred_element_type=jnp.float32,
    )
    return out_term, jnp.max(masked, axis=(0, 2)), lax.all_gather(w_proj, "dp", axis=0, tiled=True)


def any_slice(patches, ln_gain, w_qkv, w_out, w_proj, seg_ids, patch_mask, grid_hw, owners):
    tok_count, width_in = patches.shape
    head_dim = w_out.shape[0] // HEADS
    image_count = grid_hw.shape[0]
    proj_w = w_proj.shape[1]
    devices = lax.axis_size("dp")
    tokens_f = patches.astype(jnp.float32)
    row_pos, col_pos, areas, starts = token_places(seg_ids, grid_hw)
    tables = rope_tables(row_pos, col_pos, head_dim)
    image_ids = jnp.arange(image_count, dtype=jnp.int32)
    out_term, row_top, wp = plain_gathers(
        patches, ln_gain, tables, seg_ids, patch_mask, w_qkv, w_out, w_proj
    )
    member_q = seg_ids[:, None] == image_ids[None, :]
    top_logit = jnp.max(jnp.where(member_q, row_top[:, None], -1e30), axis=0)
    residual = (tokens_f + out_term).astype(jnp.bfloat16)
    merged = residual.reshape(tok_count // 4, 4 * width_in)
    projected = jnp.dot(merged, wp, preferred_element_type=jnp.float32)
    proj_bf = projected.astype(jnp.bfloat16)
    merged_seg = seg_ids.reshape(-1, 4)[:, 0]
    member_m = merged_seg[:, None] == image_ids[None, :]
    squares = jnp.sum(projected * projected, axis=1)
    totals = jnp.sum(jnp.where(member_m, squares[:, None], 0.0), axis=0)
    image_rms = jnp.sqrt(totals / (areas // 4 * proj_w).astype(jnp.float32))
    sent = send_rows(proj_bf, starts, areas, owners, devices)
    arrived = lax.all_to_all(sent, "dp", split_axis=0, concat_axis=0, tiled=True)
    return (arrived.reshape(-1, proj_w), image_rms, top_logit)


class Place:
    def __init__(self):
        me = lax.axis_index("dp")
        self.core = me % 2
        self.x = (me // 2) % 2
        self.y = (me // 4) % 2
        self.z = me // 8
        self.inner = (self.z == 1) | (self.z == 2)

    def line(self, r):
        z = self.z
        return (z, z + 1 - 2 * (z % 2), z + 2 - 4 * (z // 2), 3 - z)[r]

    def device(self, z, y, x, core):
        return ((z * 2 + y) * 2 + x) * 2 + core

    def peer(self, name):
        z, y, x, c = self.z, self.y, self.x, self.core
        if name == "x":
            return self.device(z, y, 1 - x, c)
        if name == "y":
            return self.device(z, 1 - y, x, c)
        if name == "t":
            return self.device(z, y, x, 1 - c)
        return self.device(self.line(int(name[1])), y, x, c)

    def greet(self, devices):
        barrier = pltpu.get_barrier_semaphore()
        me = lax.axis_index("dp")

        def hello(k, carry):
            other = lax.rem(me + k, devices)
            pl.semaphore_signal(barrier, inc=1, device_id=(other,), device_id_type=MESH)
            return carry

        lax.fori_loop(1, devices, hello, 0)
        pl.semaphore_wait(barrier, devices - 1)


class Wires:
    def __init__(self, place, send, recv, local):
        self.place, self.send, self.recv, self.local = place, send, recv, local
        self.used = 0
        self.locals = 0
        self.sent = []

    def copy(self, src, dst, to, only=None, slot=None):
        n = self.used
        self.used += 1
        got = n if slot is None else slot
        c = pltpu.make_async_remote_copy(
            src_ref=src, dst_ref=dst, send_sem=self.send.at[n], recv_sem=self.recv.at[got],
            device_id=(self.place.peer(to),), device_id_type=MESH)
        if only is None:
            c.start()
        else:
            pl.when(only)(c.start)
        self.sent.append((c, only))
        return got, c

    def own(self, src, dst):
        c = pltpu.make_async_copy(src, dst, self.local.at[self.locals])
        self.locals += 1
        c.start()
        return c


class Pairs:
    stages = 6

    def __init__(self, wires, first, src, dst):
        self.w, self.first, self.src, self.dst = wires, first, src, dst
        self.second = "y" if first == "x" else "x"

    def pair(self, r, far):
        p = self.w.place
        z = p.line(r)
        if self.first == "x":
            return self.dst(z, 1 - p.y if far else p.y, None)
        return self.dst(z, None, 1 - p.x if far else p.x)

    def stage(self, n):
        w, p = self.w, self.w.place
        if n == 0:
            mine = self.dst(p.z, p.y, p.x)
            self.mine = w.own(self.src, mine)
            self.from_first = w.copy(self.src, mine, self.first)[1]
        elif n == 1:
            self.mine.wait()
            self.from_first.wait_recv()
            own = self.pair(0, False)
            self.z2 = w.copy(own, own, "z2")
            self.z1 = w.copy(own, own, "z1")
            self.z3 = w.copy(own, own, "z3", only=p.inner)
            self.far = [w.copy(own, own, self.second)[1]]
        elif n == 2:
            self.z2[1].wait_recv()
            got = self.pair(2, False)
            w.copy(got, got, "z1", only=p.inner, slot=self.z3[0])
            self.spread(got)
            self.z1[1].wait_recv()
            self.spread(self.pair(1, False))
        elif n == 3:
            self.z3[1].wait_recv()
            self.spread(self.pair(3, False))
        elif n == 4:
            for copy in self.far:
                copy.wait_recv()
            whole = self.dst(None, None, None)
            self.twin = w.copy(whole, whole, "t")[1]
        elif n == 5:
            self.twin.wait_recv()

    def spread(self, got):
        self.far.append(self.w.copy(got, got, self.second)[1])


class Lines:
    stages = 6

    def __init__(self, wires, src, dst):
        self.w, self.src, self.dst = wires, src, dst

    def column(self, r, s):
        p = self.w.place
        odd = (p.z + r) % 2
        x, y = p.x, p.y
        if s == 0:
            return y, x
        if s == 1:
            return y + odd * (1 - 2 * y), x + (1 - odd) * (1 - 2 * x)
        if s == 2:
            return y + (1 - odd) * (1 - 2 * y), x + odd * (1 - 2 * x)
        return 1 - y, 1 - x

    def unit(self, r, s):
        p = self.w.place
        y, x = self.column(r, s)
        return self.dst(p.line(r), y, x)

    def side(self, r, s):
        p = self.w.place
        y, x = self.column(r, s)
        return p.device(p.z, y, x, p.core)

    def send_side(self, ref, r, s):
        w = self.w
        n = w.used
        w.used += 1
        c = pltpu.make_async_remote_copy(
            src_ref=ref, dst_ref=ref, send_sem=w.send.at[n], recv_sem=w.recv.at[n],
            device_id=(self.side(r, s),), device_id_type=MESH)
        c.start()
        w.sent.append((c, None))
        return c

    def spread(self, r):
        ref = self.unit(r, 0)
        self.s1[r] = self.send_side(ref, r, 1)
        self.s2[r] = self.send_side(ref, r, 2)

    def stage(self, n):
        w, p = self.w, self.w.place
        if n == 0:
            self.s1, self.s2, self.s3 = {}, {}, {}
            mine = self.unit(0, 0)
            self.mine = w.own(self.src, mine)
            self.z2 = w.copy(self.src, mine, "z2")
            self.z1 = w.copy(self.src, mine, "z1")
            self.z3 = w.copy(self.src, mine, "z3", only=p.inner)
        elif n == 1:
            self.mine.wait()
            self.spread(0)
            self.z2[1].wait_recv()
            got = self.unit(2, 0)
            w.copy(got, got, "z1", only=p.inner, slot=self.z3[0])
            self.spread(2)
            self.z1[1].wait_recv()
            self.spread(1)
        elif n == 2:
            self.z3[1].wait_recv()
            self.spread(3)
            for r in (0, 2):
                self.corner(r)
        elif n == 3:
            for r in (1, 3):
                self.corner(r)
        elif n == 4:
            for r in (0, 2, 1, 3):
                self.s2[r].wait_recv()
                self.s3[r].wait_recv()
            whole = self.dst(None, None, None)
            self.twin = w.copy(whole, whole, "t")[1]
        elif n == 5:
            self.twin.wait_recv()

    def corner(self, r):
        self.s1[r].wait_recv()
        ref = self.unit(r, 1)
        self.s3[r] = self.send_side(ref, r, 2)


def finish(wires):
    for c, only in wires.sent:
        if only is None:
            c.wait_send()
        else:
            pl.when(only)(c.wait_send)


class Planes:
    stages = 5

    def __init__(self, wires, src, dst):
        self.w, self.src, self.dst = wires, src, dst

    def unit(self, r):
        return self.dst(self.w.place.line(r), self.w.place.x)

    def spread(self, r):
        ref = self.unit(r)
        self.sides.append(self.w.copy(ref, ref, "x")[1])

    def stage(self, n):
        w, p = self.w, self.w.place
        if n == 0:
            self.sides = []
            mine = self.unit(0)
            self.mine = w.own(self.src, mine)
            self.z2 = w.copy(self.src, mine, "z2")
            self.z1 = w.copy(self.src, mine, "z1")
            self.z3 = w.copy(self.src, mine, "z3", only=p.inner)
        elif n == 1:
            self.mine.wait()
            self.spread(0)
            self.z2[1].wait_recv()
            got = self.unit(2)
            w.copy(got, got, "z1", only=p.inner, slot=self.z3[0])
            self.spread(2)
            self.z1[1].wait_recv()
            self.spread(1)
        elif n == 2:
            self.z3[1].wait_recv()
            self.spread(3)
        elif n == 3:
            for copy in self.sides:
                copy.wait_recv()
            whole = self.dst(None, None)
            self.twin = w.copy(whole, whole, "t")[1]
        elif n == 4:
            self.twin.wait_recv()


class PlanePairs:
    stages = 5

    def __init__(self, wires, src, dst):
        self.w, self.src, self.dst = wires, src, dst

    def stage(self, n):
        w, p = self.w, self.w.place
        if n == 0:
            mine = self.dst(p.z, p.x)
            self.mine = w.own(self.src, mine)
            self.side = w.copy(self.src, mine, "x")[1]
        elif n == 1:
            self.mine.wait()
            self.side.wait_recv()
            pair = self.dst(p.z, None)
            self.z2 = w.copy(pair, pair, "z2")
            self.z1 = w.copy(pair, pair, "z1")
            self.z3 = w.copy(pair, pair, "z3", only=p.inner)
        elif n == 2:
            self.z2[1].wait_recv()
            got = self.dst(p.line(2), None)
            w.copy(got, got, "z1", only=p.inner, slot=self.z3[0])
        elif n == 3:
            self.z1[1].wait_recv()
            self.z3[1].wait_recv()
            whole = self.dst(None, None)
            self.twin = w.copy(whole, whole, "t")[1]
        elif n == 4:
            self.twin.wait_recv()


def image_numbers(grid_ref, owner_ref, j):
    def side(i, k):
        return grid_ref[k : k + 1, i : i + 1]

    start = jnp.zeros((1, 1), jnp.int32)
    for i in range(j):
        start = start + side(i, 0) * side(i, 1)
    return start, side(j, 0) * side(j, 1), side(j, 1), owner_ref[0:1, j : j + 1]


def slot_places(shape, dim, owner, devices):
    slot = lax.broadcasted_iota(jnp.int32, shape, dim)
    corner = slot // CAP
    within = slot % CAP
    row = (within // devices) * devices + (within % devices - owner + devices) % devices
    return row, corner


def whole_kernel(
    devices,
    patches_ref,
    gain_ref,
    wqkv_ref,
    wout_ref,
    mask_ref,
    grid_ref,
    owner_ref,
    wp_ref,
    routed_ref,
    rms_ref,
    top_ref,
    wq_all,
    mine,
    wp_all,
    w_pad,
    quad,
    xs_buf,
    norm_buf,
    qk_buf,
    v_buf,
    cos_buf,
    sin_a_buf,
    sin_b_buf,
    key_buf,
    hall,
    hsend,
    csend,
    crecv,
    cown,
    squares,
    dealt,
    send,
    recv,
    local,
    quad_sem,
    deal_send,
    deal_recv,
    deal_own,
):
    place = Place()
    tokens, width = patches_ref.shape
    image = 4 * CAP
    images = tokens // image
    hw = HEADS * HEAD
    scale = HEAD ** (-0.5)

    mine[...] = jnp.zeros_like(mine)
    mine[0:ROW, 0 : 3 * hw] = wqkv_ref[...]
    mine[0:ROW, 3 * hw :] = wout_ref[...]
    place.greet(devices)

    wires = Wires(place, send, recv, local)
    half_cols = mine.shape[1] // 2
    chunks = []
    for n in range(2):
        at = n * half_cols
        pieces = []
        for kind, tiles in (("x", 4), ("y", 4), ("l", 5)):
            cols = slice(at, at + tiles * LANES)
            at += tiles * LANES

            def dst(z, y, x, cols=cols):
                z, y, x = [slice(None) if v is None else v for v in (z, y, x)]
                return wq_all.at[z, y, x, place.core, :, cols]

            src = mine.at[:, cols]
            piece = Lines(wires, src, dst) if kind == "l" else Pairs(wires, kind, src, dst)
            pieces.append(piece)
        chunks.append(pieces)
    p_chunks = csend.shape[0]
    wide = wp_ref.shape[1] // p_chunks
    for n in range(p_chunks):
        cols = slice(n * wide, (n + 1) * wide)

        def dst(z, x, cols=cols):
            z, x = [slice(None) if v is None else v for v in (z, x)]
            return wp_all.at[z, x, place.core, :, cols]

        kind = PlanePairs if n in (4,) else Planes
        chunks.append([kind(wires, wp_ref.at[:, cols], dst)])

    def front(j):
        start, area, w_image, owner = image_numbers(grid_ref, owner_ref, j)
        rows = slice(j * image, (j + 1) * image)
        row, corner = slot_places((image, 1), 0, owner, devices)
        src = jnp.where(row < area // 4, start + 4 * row + corner, -1)
        pick = (lax.broadcasted_iota(jnp.int32, (image, tokens), 1) == src).astype(BF16)
        x = jnp.dot(pick, patches_ref[...], preferred_element_type=F32)
        xs_buf[rows, :] = x.astype(BF16)
        centered = x - jnp.mean(x, axis=1, keepdims=True)
        var = jnp.mean(centered * centered, axis=1, keepdims=True)
        norm_buf[rows, :] = (centered * lax.rsqrt(var + 1e-06) * gain_ref[...][None, :]).astype(BF16)
        keys = lax.dot_general(
            jnp.broadcast_to((mask_ref[...] == 1).astype(F32), (16, tokens)).astype(BF16),
            pick,
            (((1,), (1,)), ((), ())),
            preferred_element_type=F32,
        )
        key_buf[j] = keys[0:8, :]
        half_w = (w_image // 2).astype(F32)
        row_f = row.astype(F32)
        down = jnp.floor((row_f + 0.5) / half_w)
        across = row_f - down * half_w
        bottom = (corner // 2).astype(F32)
        right = (corner % 2).astype(F32)
        row_pos = 2.0 * down + bottom
        col_pos = 2.0 * across + right
        lane = lax.broadcasted_iota(jnp.int32, (1, LANES), 1)
        part = lane // QUARTER
        theta = jnp.exp((lane % QUARTER).astype(F32) * (-math.log(100.0) / QUARTER))
        angles = jnp.where(part < 2, row_pos, col_pos) * theta
        cosine = jnp.cos(angles)
        sine = jnp.sin(angles)
        cos_buf[rows, :] = jnp.where(part < 4, cosine, 0.0)
        sin_a_buf[rows, :] = jnp.where((part == 0) | (part == 2), -sine, 0.0)
        sin_b_buf[rows, :] = jnp.where((part == 1) | (part == 3), sine, 0.0)

    def spread_heads(half):
        cols = slice(half * half_cols, (half + 1) * half_cols)
        count = half_cols // HEAD

        def load(g, slot):
            return pltpu.make_async_copy(
                wq_all.at[g // 2, g % 2, :, :, :, cols], quad.at[slot], quad_sem.at[slot]
            )

        load(0, 0).start()

        def body(g, carry):
            slot = g % 2

            @pl.when(g < 7)
            def _():
                load(g + 1, 1 - slot).start()

            load(g, slot).wait()
            block = jnp.concatenate(
                [quad[slot, i // 2, i % 2, 0:ROW, :].astype(F32) for i in range(4)], axis=0
            )
            rows = pl.ds(pl.multiple_of(g * 4 * ROW, 16), 4 * ROW)
            lane = lax.broadcasted_iota(jnp.int32, (4 * ROW, LANES), 1)
            for h in range(count):
                tile = HEAD * h // LANES * LANES
                off = HEAD * h - tile
                if off + HEAD <= LANES:
                    val = block[:, tile : tile + LANES]
                    if off:
                        val = pltpu.roll(val, LANES - off, 1)
                else:
                    val = jnp.where(
                        lane < LANES - off,
                        pltpu.roll(block[:, tile : tile + LANES], LANES - off, 1),
                        pltpu.roll(block[:, tile + LANES : tile + 2 * LANES], LANES - off, 1),
                    )
                at = (half * count + h) * LANES
                w_pad[rows, at : at + LANES] = jnp.where(lane < HEAD, val, 0.0).astype(BF16)
            return carry

        lax.fori_loop(0, 8, body, 0)

    wide_heads = HEADS * LANES

    def queries_keys(i):
        rows = slice(i * image, (i + 1) * image)

        def body(n, carry):
            cols = pl.ds(pl.multiple_of(n * 512, 512), 512)
            mixed = jnp.dot(norm_buf[rows, :], w_pad[:, cols], preferred_element_type=F32)
            cosine, sin_a, sin_b = cos_buf[rows, :], sin_a_buf[rows, :], sin_b_buf[rows, :]
            outs = []
            for h in range(4):
                val = mixed[:, h * LANES : (h + 1) * LANES]
                val = (
                    val * cosine
                    + pltpu.roll(val, LANES - QUARTER, 1) * sin_a
                    + pltpu.roll(val, QUARTER, 1) * sin_b
                )
                outs.append(val.astype(BF16))
            qk_buf[rows, cols] = jnp.concatenate(outs, axis=1)
            return carry

        lax.fori_loop(0, 2 * wide_heads // 512, body, 0)

    def values(i):
        rows = slice(i * image, (i + 1) * image)
        for n in range(wide_heads // 512):
            cols = slice(n * 512, (n + 1) * 512)
            w_cols = slice(2 * wide_heads + n * 512, 2 * wide_heads + (n + 1) * 512)
            mixed = jnp.dot(norm_buf[rows, :], w_pad[:, w_cols], preferred_element_type=F32)
            v_buf[rows, cols] = mixed.astype(BF16)

    exchanged = []

    def attend(j):
        start, area, w_image, owner = image_numbers(grid_ref, owner_ref, j)
        rows = slice(j * image, (j + 1) * image)
        same = lax.broadcasted_iota(jnp.int32, (image, image), 0) == lax.broadcasted_iota(
            jnp.int32, (image, image), 1
        )
        bias = jnp.where((key_buf[j, 0:1, :] > 0.5) | same, 0.0, -1e30)
        best = jnp.full((image, 1), -1e30, F32)
        row, _ = slot_places((image, 1), 0, owner, devices)
        valid = row < area // 4
        for h in range(HEADS):
            lanes = slice(h * LANES, (h + 1) * LANES)
            k_lanes = slice(wide_heads + h * LANES, wide_heads + (h + 1) * LANES)
            scores = lax.dot_general(
                qk_buf[rows, lanes],
                qk_buf[rows, k_lanes],
                (((1,), (1,)), ((), ())),
                preferred_element_type=F32,
            )
            scores = scores * scale + bias
            top = jnp.max(scores, axis=1, keepdims=True)
            best = jnp.maximum(best, top)
            expo = jnp.exp(scores - top)
            total = jnp.sum(expo, axis=1, keepdims=True)
            got = jnp.dot(expo.astype(BF16), v_buf[rows, lanes], preferred_element_type=F32)
            qk_buf[rows, lanes] = (got * jnp.where(valid, 1.0 / total, 0.0)).astype(BF16)
        best = jnp.where(valid, best, -1e30)
        top_ref[j : j + 1, :] = jnp.broadcast_to(
            jnp.max(best, axis=0, keepdims=True), (1, LANES)
        )
        out = lax.dot_general(
            qk_buf[rows, :wide_heads],
            w_pad[:, 3 * wide_heads :],
            (((1,), (1,)), ((), ())),
            preferred_element_type=F32,
        )
        res = out + xs_buf[rows, :].astype(F32)
        turned = pltpu.roll(res, width // 2, 1)
        upper = place.y == 0
        own = jnp.where(upper, res, turned)[:, : width // 2].astype(BF16)
        other = jnp.where(upper, turned, res)[:, : width // 2].astype(BF16)
        at = j * CAP
        for c in range(4):
            hall[c, at : at + CAP, :] = own[c * CAP : (c + 1) * CAP, :]
            hsend[c, at : at + CAP, :] = other[c * CAP : (c + 1) * CAP, :]
        merged_rows = hsend.shape[1]
        exchanged.append(
            wires.copy(
                hsend.at[:, at : at + CAP, :],
                hall.at[:, merged_rows + at : merged_rows + at + CAP, :],
                "y",
            )[1]
        )

    partials = {}

    def project(n):
        if n == 0:
            for c in exchanged:
                c.wait_recv()
        merged_rows = hsend.shape[1]
        cols = slice(n * wide, (n + 1) * wide)
        total = jnp.zeros((2 * merged_rows, wide), F32)
        for c in range(4):
            total = total + jnp.dot(
                hall[c],
                wp_all[c, :, :, :, cols].reshape(width // 2, wide),
                preferred_element_type=F32,
            )
        cown[:, cols] = total[:merged_rows]
        csend[n] = total[merged_rows:].astype(BF16)
        partials[n] = wires.copy(csend.at[n], crecv.at[n], "y")[1]

    def complete(n):
        partials[n].wait_recv()
        merged_rows = hsend.shape[1]
        cols = slice(n * wide, (n + 1) * wide)
        done = cown[:, cols] + crecv[n].astype(F32)
        sq = jnp.sum(done * done, axis=1, keepdims=True)
        if n == 0:
            squares[...] = jnp.broadcast_to(sq, squares.shape)
        else:
            squares[...] += jnp.broadcast_to(sq, squares.shape)
        slots = merged_rows // devices
        out_row = lax.broadcasted_iota(jnp.int32, (merged_rows, merged_rows), 0)
        in_row = lax.broadcasted_iota(jnp.int32, (merged_rows, merged_rows), 1)
        deal = (in_row == (out_row % slots) * devices + out_row // slots).astype(BF16)
        out = jnp.dot(deal, done.astype(BF16), preferred_element_type=F32)
        dealt[:, :, cols] = out.reshape(devices, slots, wide).astype(BF16)

    me = lax.axis_index("dp")
    deals = [slice(lo * wide, hi * wide) for lo, hi in ((0, 3), (3, 6), (6, 7), (7, 8))]

    def deal_out(n):
        cols = deals[n]
        pltpu.make_async_copy(
            dealt.at[me, :, cols], routed_ref.at[me, :, cols], deal_own.at[n]
        ).start()

        def give(k, carry):
            to = lax.rem(me + k, devices)
            pltpu.make_async_remote_copy(
                src_ref=dealt.at[to, :, cols],
                dst_ref=routed_ref.at[me, :, cols],
                send_sem=deal_send.at[n],
                recv_sem=deal_recv.at[n],
                device_id=(to,),
                device_id_type=MESH,
            ).start()
            return carry

        lax.fori_loop(1, devices, give, 0)

    def dealt_all():
        for n, cols in enumerate(deals):
            others = routed_ref.at[pl.ds(0, devices - 1), :, cols]
            pltpu.make_async_copy(others, others, deal_recv.at[n]).wait()
            given = dealt.at[pl.ds(0, devices - 1), :, cols]
            pltpu.make_async_copy(given, given, deal_send.at[n]).wait()
            pltpu.make_async_copy(
                dealt.at[me, :, cols], routed_ref.at[me, :, cols], deal_own.at[n]
            ).wait()

    work = {
        0: [lambda: front(0)],
        1: [lambda: front(1)],
        2: [lambda: front(2)],
        3: [lambda: front(3)],
        5: [lambda: spread_heads(0)],
        6: [lambda: queries_keys(0)],
        7: [lambda: spread_heads(1)],
        8: [lambda: values(0), lambda: attend(0)],
        9: [lambda: queries_keys(1), lambda: values(1), lambda: attend(1)],
        10: [lambda: queries_keys(2), lambda: values(2), lambda: attend(2)],
        11: [lambda: queries_keys(3), lambda: values(3), lambda: attend(3)],
    }
    ahead = {
        15: [lambda: project(0), lambda: project(1), lambda: project(2)],
        16: [lambda: project(3), lambda: complete(0), lambda: complete(1)],
        17: [lambda: project(4), lambda: complete(2), lambda: deal_out(0), lambda: complete(3)],
        18: [lambda: project(5), lambda: complete(4)],
        19: [lambda: project(6), lambda: complete(5), lambda: deal_out(1)],
        20: [lambda: project(7), lambda: complete(6), lambda: deal_out(2)],
        21: [lambda: complete(7), lambda: deal_out(3)],
    }
    when = [
        [0, 1, 2, 3, 4, 5],
        [2, 3, 4, 5, 6, 7],
        [4, 6, 7, 9, 10],
        [6, 8, 9, 11, 12],
        [7, 9, 10, 13, 14],
        [9, 11, 12, 14, 15],
        [10, 11, 13, 15, 16],
        [11, 13, 14, 16, 17],
        [12, 14, 15, 17, 18],
        [13, 15, 16, 18, 19],
    ]
    for step in range(max(ahead) + 1):
        for task in ahead.get(step, ()):
            task()
        for steps, pieces in zip(when, chunks):
            for stage, at in enumerate(steps):
                if at == step:
                    for piece in pieces:
                        piece.stage(stage)
        for task in work.get(step, ()):
            task()
    for j in range(images):
        area = image_numbers(grid_ref, owner_ref, j)[1]
        total = jnp.sum(squares[j * CAP : (j + 1) * CAP, :], axis=0, keepdims=True)
        count = (area // 4 * wp_ref.shape[1]).astype(F32)
        rms_ref[j : j + 1, :] = jnp.sqrt(total / count)
    finish(wires)
    dealt_all()


def one_kernel(patches, ln_gain, w_qkv, w_out, w_proj, patch_mask, grid_hw, owners, devices):
    tokens, width = patches.shape
    proj_w = w_proj.shape[1]
    merged = tokens // 4
    images = grid_hw.shape[0]
    vmem = pl.BlockSpec(memory_space=pltpu.VMEM)
    hbm = pl.BlockSpec(memory_space=pl.ANY)
    pad_row = 56
    cols = 4 * HEADS * HEAD
    wide = HEADS * LANES
    p_chunks = 8
    scratch = [
        pltpu.VMEM((pad_row, cols), BF16),
        pltpu.VMEM((4, 2, 2) + w_proj.shape, BF16),
        pltpu.VMEM((width, 4 * wide), BF16),
        pltpu.VMEM((2, 2, 2, pad_row, cols // 2), BF16),
        pltpu.VMEM((tokens, width), BF16),
        pltpu.VMEM((tokens, width), BF16),
        pltpu.VMEM((tokens, 2 * wide), BF16),
        pltpu.VMEM((tokens, wide), BF16),
        pltpu.VMEM((tokens, LANES), F32),
        pltpu.VMEM((tokens, LANES), F32),
        pltpu.VMEM((tokens, LANES), F32),
        pltpu.VMEM((images, 8, 4 * CAP), F32),
        pltpu.VMEM((4, 2 * merged, width // 2), BF16),
        pltpu.VMEM((4, merged, width // 2), BF16),
        pltpu.VMEM((p_chunks, merged, proj_w // p_chunks), BF16),
        pltpu.VMEM((p_chunks, merged, proj_w // p_chunks), BF16),
        pltpu.VMEM((merged, proj_w), F32),
        pltpu.VMEM((merged, LANES), F32),
        pltpu.VMEM((devices, merged // devices, proj_w), BF16),
        pltpu.SemaphoreType.DMA((155,)),
        pltpu.SemaphoreType.DMA((155,)),
        pltpu.SemaphoreType.DMA((14,)),
        pltpu.SemaphoreType.DMA((2,)),
        pltpu.SemaphoreType.DMA((4,)),
        pltpu.SemaphoreType.DMA((4,)),
        pltpu.SemaphoreType.DMA((4,)),
    ]
    return pl.pallas_call(
        functools.partial(whole_kernel, devices),
        out_shape=(
            jax.ShapeDtypeStruct((devices, merged // devices, proj_w), BF16),
            jax.ShapeDtypeStruct((8, LANES), F32),
            jax.ShapeDtypeStruct((8, LANES), F32),
            jax.ShapeDtypeStruct((4, 2, 2, 2, pad_row, cols), BF16),
        ),
        in_specs=[vmem] * 7 + [hbm],
        out_specs=(hbm, vmem, vmem, hbm),
        scratch_shapes=scratch,
        compiler_params=pltpu.CompilerParams(
            collective_id=1, has_side_effects=True, vmem_limit_bytes=63 * 1024 * 1024
        ),
    )(
        patches,
        ln_gain,
        w_qkv,
        w_out.T,
        patch_mask[None, :],
        grid_hw.T,
        owners[None, :],
        w_proj,
    )


def this_slice(patches, ln_gain, w_qkv, w_out, w_proj, seg_ids, patch_mask, grid_hw, owners):
    devices = lax.axis_size("dp")
    images = grid_hw.shape[0]
    routed, rms, top, _ = one_kernel(
        patches, ln_gain, w_qkv, w_out, w_proj, patch_mask, grid_hw, owners, devices
    )
    return routed.reshape(-1, w_proj.shape[1]), rms[:images, 0], top[:images, 0]


def on_device(*args):
    path = this_slice if lax.axis_size("dp") == 32 else any_slice
    return path(*args)


def solution(mesh):
    return jax.shard_map(
        on_device,
        mesh=mesh,
        in_specs=(
            P("dp", None),
            P(),
            P("dp", None),
            P(None, "dp"),
            P("dp", None),
            P("dp"),
            P("dp"),
            P("dp", None),
            P("dp"),
        ),
        out_specs=(P("dp", None), P("dp"), P("dp")),
        check_vma=False,
    )
```

```python
import functools
import math

import jax
import jax.numpy as jnp
from jax import lax
from jax.experimental import pallas as pl
from jax.experimental.pallas import tpu as pltpu
from jax.sharding import PartitionSpec as P

HEADS = 8
CAP = 64
LANES = 128
HEAD = 104
QUARTER = 26
ROW = 52
MESH = pl.DeviceIdType.MESH
F32 = jnp.float32
BF16 = jnp.bfloat16


def token_places(seg_row, grid_rows):
    heights = grid_rows[:, 0]
    widths = grid_rows[:, 1]
    areas = heights * widths
    order = jnp.arange(areas.shape[0])
    ends_at = jnp.sum(jnp.where(order[None, :] <= order[:, None], areas[None, :], 0), axis=1)
    starts = ends_at - areas
    image_count = grid_rows.shape[0]
    member = seg_row[:, None] == jnp.arange(image_count, dtype=jnp.int32)[None, :]
    start_tok = jnp.sum(jnp.where(member, starts[None, :], 0), axis=1)
    half_w = jnp.maximum(jnp.sum(jnp.where(member, (widths // 2)[None, :], 0), axis=1), 1)
    offset = jnp.arange(seg_row.shape[0], dtype=jnp.int32) - start_tok
    window = offset // 4
    corner = offset % 4
    row_pos = 2 * (window // half_w) + corner // 2
    col_pos = 2 * (window % half_w) + corner % 2
    return (row_pos.astype(jnp.float32), col_pos.astype(jnp.float32), areas, starts)


def rope_tables(row_pos, col_pos, head_dim):
    quarter = head_dim // 4
    lane = jnp.arange(LANES, dtype=jnp.int32)
    theta = 100.0 ** (-(lane % quarter).astype(jnp.float32) / quarter)
    part = lane // quarter
    pos = jnp.where(part[None, :] < 2, row_pos[:, None], col_pos[:, None])
    angles = pos * theta[None, :]
    cosine = jnp.cos(angles)
    sine = jnp.sin(angles)
    first = (part == 0) | (part == 2)
    second = (part == 1) | (part == 3)
    return (
        cosine,
        jnp.where(first[None, :], -sine, 0.0),
        jnp.where(second[None, :], sine, 0.0),
    )


def send_rows(proj_bf, starts, areas, owner_row, device_count):
    merged_rows = proj_bf.shape[0]
    wrap_count = (CAP + device_count - 1) // device_count
    dest_ids = jnp.arange(device_count, dtype=jnp.int32)[:, None, None]
    wrap_ids = jnp.arange(wrap_count, dtype=jnp.int32)[None, None, :]
    owner_here = owner_row[None, :, None]
    row_within = wrap_ids * device_count + (dest_ids - owner_here) % device_count
    row_total = (areas // 4)[None, :, None]
    first_row = (starts // 4)[None, :, None]
    picked = jnp.where(row_within < row_total, first_row + row_within, merged_rows)
    padded = jnp.concatenate([proj_bf, jnp.zeros((1, proj_bf.shape[1]), proj_bf.dtype)], axis=0)
    return padded[picked]


def plain_gathers(patches, ln_gain, tables, seg_ids, patch_mask, w_qkv, w_out, w_proj):
    tok_count = patches.shape[0]
    tokens_f = patches.astype(jnp.float32)
    mean_row = jnp.mean(tokens_f, axis=-1, keepdims=True)
    centered = tokens_f - mean_row
    var_row = jnp.mean(centered * centered, axis=-1, keepdims=True)
    normed = (centered * lax.rsqrt(var_row + 1e-06) * ln_gain).astype(jnp.bfloat16)
    hidden_w = w_out.shape[0]
    head_dim = hidden_w // HEADS
    quarter = head_dim // 4
    mixed = jnp.dot(
        normed, lax.all_gather(w_qkv, "dp", axis=0, tiled=True), preferred_element_type=jnp.float32
    )
    shape_three = (tok_count, HEADS, head_dim)
    cosine, sin_a, sin_b = [t[:, None, :head_dim] for t in tables]

    def rotate(val):
        return (
            val * cosine
            + jnp.roll(val, -quarter, axis=2) * sin_a
            + jnp.roll(val, quarter, axis=2) * sin_b
        ).astype(jnp.bfloat16)

    queries = rotate(mixed[:, :hidden_w].reshape(shape_three))
    key_rows = rotate(mixed[:, hidden_w : 2 * hidden_w].reshape(shape_three))
    values = mixed[:, 2 * hidden_w :].reshape(shape_three).astype(jnp.bfloat16)
    scores = jnp.einsum("qhd,khd->hqk", queries, key_rows, preferred_element_type=jnp.float32)
    idx = jnp.arange(tok_count, dtype=jnp.int32)
    allowed = (seg_ids[:, None] == seg_ids[None, :]) & (
        (patch_mask[None, :] == 1) | (idx[:, None] == idx[None, :])
    )
    masked = jnp.where(allowed[None], scores * head_dim ** (-0.5), -1e30)
    weights = jax.nn.softmax(masked, axis=-1).astype(jnp.bfloat16)
    attended = jnp.einsum("hqk,khd->qhd", weights, values, preferred_element_type=jnp.float32)
    attended = attended.astype(jnp.bfloat16).reshape(tok_count, hidden_w)
    out_term = jnp.dot(
        attended,
        lax.all_gather(w_out, "dp", axis=1, tiled=True),
        preferred_element_type=jnp.float32,
    )
    return out_term, jnp.max(masked, axis=(0, 2)), lax.all_gather(w_proj, "dp", axis=0, tiled=True)


def any_slice(patches, ln_gain, w_qkv, w_out, w_proj, seg_ids, patch_mask, grid_hw, owners):
    tok_count, width_in = patches.shape
    head_dim = w_out.shape[0] // HEADS
    image_count = grid_hw.shape[0]
    proj_w = w_proj.shape[1]
    devices = lax.axis_size("dp")
    tokens_f = patches.astype(jnp.float32)
    row_pos, col_pos, areas, starts = token_places(seg_ids, grid_hw)
    tables = rope_tables(row_pos, col_pos, head_dim)
    image_ids = jnp.arange(image_count, dtype=jnp.int32)
    out_term, row_top, wp = plain_gathers(
        patches, ln_gain, tables, seg_ids, patch_mask, w_qkv, w_out, w_proj
    )
    member_q = seg_ids[:, None] == image_ids[None, :]
    top_logit = jnp.max(jnp.where(member_q, row_top[:, None], -1e30), axis=0)
    residual = (tokens_f + out_term).astype(jnp.bfloat16)
    merged = residual.reshape(tok_count // 4, 4 * width_in)
    projected = jnp.dot(merged, wp, preferred_element_type=jnp.float32)
    proj_bf = projected.astype(jnp.bfloat16)
    merged_seg = seg_ids.reshape(-1, 4)[:, 0]
    member_m = merged_seg[:, None] == image_ids[None, :]
    squares = jnp.sum(projected * projected, axis=1)
    totals = jnp.sum(jnp.where(member_m, squares[:, None], 0.0), axis=0)
    image_rms = jnp.sqrt(totals / (areas // 4 * proj_w).astype(jnp.float32))
    sent = send_rows(proj_bf, starts, areas, owners, devices)
    arrived = lax.all_to_all(sent, "dp", split_axis=0, concat_axis=0, tiled=True)
    return (arrived.reshape(-1, proj_w), image_rms, top_logit)


class Place:
    def __init__(self):
        me = lax.axis_index("dp")
        self.core = me % 2
        self.x = (me // 2) % 2
        self.y = (me // 4) % 2
        self.z = me // 8
        self.inner = (self.z == 1) | (self.z == 2)

    def line(self, r):
        z = self.z
        return (z, z + 1 - 2 * (z % 2), z + 2 - 4 * (z // 2), 3 - z)[r]

    def device(self, z, y, x, core):
        return ((z * 2 + y) * 2 + x) * 2 + core

    def peer(self, name):
        z, y, x, c = self.z, self.y, self.x, self.core
        if name == "x":
            return self.device(z, y, 1 - x, c)
        if name == "y":
            return self.device(z, 1 - y, x, c)
        if name == "t":
            return self.device(z, y, x, 1 - c)
        return self.device(self.line(int(name[1])), y, x, c)

    def greet(self, devices):
        barrier = pltpu.get_barrier_semaphore()
        me = lax.axis_index("dp")

        def hello(k, carry):
            other = lax.rem(me + k, devices)
            pl.semaphore_signal(barrier, inc=1, device_id=(other,), device_id_type=MESH)
            return carry

        lax.fori_loop(1, devices, hello, 0)
        pl.semaphore_wait(barrier, devices - 1)


class Wires:
    def __init__(self, place, send, recv, local):
        self.place, self.send, self.recv, self.local = place, send, recv, local
        self.used = 0
        self.locals = 0
        self.sent = []

    def copy(self, src, dst, to, only=None, slot=None):
        n = self.used
        self.used += 1
        got = n if slot is None else slot
        c = pltpu.make_async_remote_copy(
            src_ref=src, dst_ref=dst, send_sem=self.send.at[n], recv_sem=self.recv.at[got],
            device_id=(self.place.peer(to),), device_id_type=MESH)
        if only is None:
            c.start()
        else:
            pl.when(only)(c.start)
        self.sent.append((c, only))
        return got, c

    def own(self, src, dst):
        c = pltpu.make_async_copy(src, dst, self.local.at[self.locals])
        self.locals += 1
        c.start()
        return c


class Pairs:
    stages = 6

    def __init__(self, wires, first, src, dst):
        self.w, self.first, self.src, self.dst = wires, first, src, dst
        self.second = "y" if first == "x" else "x"

    def pair(self, r, far):
        p = self.w.place
        z = p.line(r)
        if self.first == "x":
            return self.dst(z, 1 - p.y if far else p.y, None)
        return self.dst(z, None, 1 - p.x if far else p.x)

    def stage(self, n):
        w, p = self.w, self.w.place
        if n == 0:
            mine = self.dst(p.z, p.y, p.x)
            self.mine = w.own(self.src, mine)
            self.from_first = w.copy(self.src, mine, self.first)[1]
        elif n == 1:
            self.mine.wait()
            self.from_first.wait_recv()
            own = self.pair(0, False)
            self.z2 = w.copy(own, own, "z2")
            self.z1 = w.copy(own, own, "z1")
            self.z3 = w.copy(own, own, "z3", only=p.inner)
            self.far = [w.copy(own, own, self.second)[1]]
        elif n == 2:
            self.z2[1].wait_recv()
            got = self.pair(2, False)
            w.copy(got, got, "z1", only=p.inner, slot=self.z3[0])
            self.spread(got)
            self.z1[1].wait_recv()
            self.spread(self.pair(1, False))
        elif n == 3:
            self.z3[1].wait_recv()
            self.spread(self.pair(3, False))
        elif n == 4:
            for copy in self.far:
                copy.wait_recv()
            whole = self.dst(None, None, None)
            self.twin = w.copy(whole, whole, "t")[1]
        elif n == 5:
            self.twin.wait_recv()

    def spread(self, got):
        self.far.append(self.w.copy(got, got, self.second)[1])


class Lines:
    stages = 6

    def __init__(self, wires, src, dst):
        self.w, self.src, self.dst = wires, src, dst

    def column(self, r, s):
        p = self.w.place
        odd = (p.z + r) % 2
        x, y = p.x, p.y
        if s == 0:
            return y, x
        if s == 1:
            return y + odd * (1 - 2 * y), x + (1 - odd) * (1 - 2 * x)
        if s == 2:
            return y + (1 - odd) * (1 - 2 * y), x + odd * (1 - 2 * x)
        return 1 - y, 1 - x

    def unit(self, r, s):
        p = self.w.place
        y, x = self.column(r, s)
        return self.dst(p.line(r), y, x)

    def side(self, r, s):
        p = self.w.place
        y, x = self.column(r, s)
        return p.device(p.z, y, x, p.core)

    def send_side(self, ref, r, s):
        w = self.w
        n = w.used
        w.used += 1
        c = pltpu.make_async_remote_copy(
            src_ref=ref, dst_ref=ref, send_sem=w.send.at[n], recv_sem=w.recv.at[n],
            device_id=(self.side(r, s),), device_id_type=MESH)
        c.start()
        w.sent.append((c, None))
        return c

    def spread(self, r):
        ref = self.unit(r, 0)
        self.s1[r] = self.send_side(ref, r, 1)
        self.s2[r] = self.send_side(ref, r, 2)

    def stage(self, n):
        w, p = self.w, self.w.place
        if n == 0:
            self.s1, self.s2, self.s3 = {}, {}, {}
            mine = self.unit(0, 0)
            self.mine = w.own(self.src, mine)
            self.z2 = w.copy(self.src, mine, "z2")
            self.z1 = w.copy(self.src, mine, "z1")
            self.z3 = w.copy(self.src, mine, "z3", only=p.inner)
        elif n == 1:
            self.mine.wait()
            self.spread(0)
            self.z2[1].wait_recv()
            got = self.unit(2, 0)
            w.copy(got, got, "z1", only=p.inner, slot=self.z3[0])
            self.spread(2)
            self.z1[1].wait_recv()
            self.spread(1)
        elif n == 2:
            self.z3[1].wait_recv()
            self.spread(3)
            for r in (0, 2):
                self.corner(r)
        elif n == 3:
            for r in (1, 3):
                self.corner(r)
        elif n == 4:
            for r in (0, 2, 1, 3):
                self.s2[r].wait_recv()
                self.s3[r].wait_recv()
            whole = self.dst(None, None, None)
            self.twin = w.copy(whole, whole, "t")[1]
        elif n == 5:
            self.twin.wait_recv()

    def corner(self, r):
        self.s1[r].wait_recv()
        ref = self.unit(r, 1)
        self.s3[r] = self.send_side(ref, r, 2)


def finish(wires):
    for c, only in wires.sent:
        if only is None:
            c.wait_send()
        else:
            pl.when(only)(c.wait_send)


class Planes:
    stages = 5

    def __init__(self, wires, src, dst):
        self.w, self.src, self.dst = wires, src, dst

    def unit(self, r):
        return self.dst(self.w.place.line(r), self.w.place.x)

    def spread(self, r):
        ref = self.unit(r)
        self.sides.append(self.w.copy(ref, ref, "x")[1])

    def stage(self, n):
        w, p = self.w, self.w.place
        if n == 0:
            self.sides = []
            mine = self.unit(0)
            self.mine = w.own(self.src, mine)
            self.z2 = w.copy(self.src, mine, "z2")
            self.z1 = w.copy(self.src, mine, "z1")
            self.z3 = w.copy(self.src, mine, "z3", only=p.inner)
        elif n == 1:
            self.mine.wait()
            self.spread(0)
            self.z2[1].wait_recv()
            got = self.unit(2)
            w.copy(got, got, "z1", only=p.inner, slot=self.z3[0])
            self.spread(2)
            self.z1[1].wait_recv()
            self.spread(1)
        elif n == 2:
            self.z3[1].wait_recv()
            self.spread(3)
        elif n == 3:
            for copy in self.sides:
                copy.wait_recv()
            whole = self.dst(None, None)
            self.twin = w.copy(whole, whole, "t")[1]
        elif n == 4:
            self.twin.wait_recv()


class PlanePairs:
    stages = 5

    def __init__(self, wires, src, dst):
        self.w, self.src, self.dst = wires, src, dst

    def stage(self, n):
        w, p = self.w, self.w.place
        if n == 0:
            mine = self.dst(p.z, p.x)
            self.mine = w.own(self.src, mine)
            self.side = w.copy(self.src, mine, "x")[1]
        elif n == 1:
            self.mine.wait()
            self.side.wait_recv()
            pair = self.dst(p.z, None)
            self.z2 = w.copy(pair, pair, "z2")
            self.z1 = w.copy(pair, pair, "z1")
            self.z3 = w.copy(pair, pair, "z3", only=p.inner)
        elif n == 2:
            self.z2[1].wait_recv()
            got = self.dst(p.line(2), None)
            w.copy(got, got, "z1", only=p.inner, slot=self.z3[0])
        elif n == 3:
            self.z1[1].wait_recv()
            self.z3[1].wait_recv()
            whole = self.dst(None, None)
            self.twin = w.copy(whole, whole, "t")[1]
        elif n == 4:
            self.twin.wait_recv()


def image_numbers(grid_ref, owner_ref, j):
    def side(i, k):
        return grid_ref[k : k + 1, i : i + 1]

    start = jnp.zeros((1, 1), jnp.int32)
    for i in range(j):
        start = start + side(i, 0) * side(i, 1)
    return start, side(j, 0) * side(j, 1), side(j, 1), owner_ref[0:1, j : j + 1]


def slot_places(shape, dim, owner, devices):
    slot = lax.broadcasted_iota(jnp.int32, shape, dim)
    corner = slot // CAP
    within = slot % CAP
    row = (within // devices) * devices + (within % devices - owner + devices) % devices
    return row, corner


def whole_kernel(
    devices,
    patches_ref,
    gain_ref,
    wqkv_ref,
    wout_ref,
    mask_ref,
    grid_ref,
    owner_ref,
    wp_ref,
    routed_ref,
    rms_ref,
    top_ref,
    wq_all,
    mine,
    wp_all,
    w_pad,
    quad,
    xs_buf,
    norm_buf,
    qk_buf,
    v_buf,
    cos_buf,
    sin_a_buf,
    sin_b_buf,
    key_buf,
    hall,
    hsend,
    csend,
    crecv,
    cown,
    squares,
    dealt,
    send,
    recv,
    local,
    quad_sem,
    deal_send,
    deal_recv,
    deal_own,
):
    place = Place()
    tokens, width = patches_ref.shape
    image = 4 * CAP
    images = tokens // image
    hw = HEADS * HEAD
    scale = HEAD ** (-0.5)

    mine[...] = jnp.zeros_like(mine)
    mine[0:ROW, 0 : 3 * hw] = wqkv_ref[...]
    mine[0:ROW, 3 * hw :] = wout_ref[...]
    place.greet(devices)

    wires = Wires(place, send, recv, local)
    half_cols = mine.shape[1] // 2
    chunks = []
    for n in range(2):
        at = n * half_cols
        pieces = []
        for kind, tiles in (("x", 4), ("y", 4), ("l", 5)):
            cols = slice(at, at + tiles * LANES)
            at += tiles * LANES

            def dst(z, y, x, cols=cols):
                z, y, x = [slice(None) if v is None else v for v in (z, y, x)]
                return wq_all.at[z, y, x, place.core, :, cols]

            src = mine.at[:, cols]
            piece = Lines(wires, src, dst) if kind == "l" else Pairs(wires, kind, src, dst)
            pieces.append(piece)
        chunks.append(pieces)
    p_chunks = csend.shape[0]
    wide = wp_ref.shape[1] // p_chunks
    for n in range(p_chunks):
        cols = slice(n * wide, (n + 1) * wide)

        def dst(z, x, cols=cols):
            z, x = [slice(None) if v is None else v for v in (z, x)]
            return wp_all.at[z, x, place.core, :, cols]

        kind = PlanePairs if n in (4,) else Planes
        chunks.append([kind(wires, wp_ref.at[:, cols], dst)])

    def front(j):
        start, area, w_image, owner = image_numbers(grid_ref, owner_ref, j)
        rows = slice(j * image, (j + 1) * image)
        row, corner = slot_places((image, 1), 0, owner, devices)
        src = jnp.where(row < area // 4, start + 4 * row + corner, -1)
        pick = (lax.broadcasted_iota(jnp.int32, (image, tokens), 1) == src).astype(BF16)
        x = jnp.dot(pick, patches_ref[...], preferred_element_type=F32)
        xs_buf[rows, :] = x.astype(BF16)
        centered = x - jnp.mean(x, axis=1, keepdims=True)
        var = jnp.mean(centered * centered, axis=1, keepdims=True)
        norm_buf[rows, :] = (centered * lax.rsqrt(var + 1e-06) * gain_ref[...][None, :]).astype(BF16)
        keys = lax.dot_general(
            jnp.broadcast_to((mask_ref[...] == 1).astype(F32), (16, tokens)).astype(BF16),
            pick,
            (((1,), (1,)), ((), ())),
            preferred_element_type=F32,
        )
        key_buf[j] = keys[0:8, :]
        half_w = (w_image // 2).astype(F32)
        row_f = row.astype(F32)
        down = jnp.floor((row_f + 0.5) / half_w)
        across = row_f - down * half_w
        bottom = (corner // 2).astype(F32)
        right = (corner % 2).astype(F32)
        row_pos = 2.0 * down + bottom
        col_pos = 2.0 * across + right
        lane = lax.broadcasted_iota(jnp.int32, (1, LANES), 1)
        part = lane // QUARTER
        theta = jnp.exp((lane % QUARTER).astype(F32) * (-math.log(100.0) / QUARTER))
        angles = jnp.where(part < 2, row_pos, col_pos) * theta
        cosine = jnp.cos(angles)
        sine = jnp.sin(angles)
        cos_buf[rows, :] = jnp.where(part < 4, cosine, 0.0)
        sin_a_buf[rows, :] = jnp.where((part == 0) | (part == 2), -sine, 0.0)
        sin_b_buf[rows, :] = jnp.where((part == 1) | (part == 3), sine, 0.0)

    def spread_heads(half):
        cols = slice(half * half_cols, (half + 1) * half_cols)
        count = half_cols // HEAD

        def load(g, slot):
            return pltpu.make_async_copy(
                wq_all.at[g // 2, g % 2, :, :, :, cols], quad.at[slot], quad_sem.at[slot]
            )

        load(0, 0).start()

        def body(g, carry):
            slot = g % 2

            @pl.when(g < 7)
            def _():
                load(g + 1, 1 - slot).start()

            load(g, slot).wait()
            block = jnp.concatenate(
                [quad[slot, i // 2, i % 2, 0:ROW, :].astype(F32) for i in range(4)], axis=0
            )
            rows = pl.ds(pl.multiple_of(g * 4 * ROW, 16), 4 * ROW)
            lane = lax.broadcasted_iota(jnp.int32, (4 * ROW, LANES), 1)
            for h in range(count):
                tile = HEAD * h // LANES * LANES
                off = HEAD * h - tile
                if off + HEAD <= LANES:
                    val = block[:, tile : tile + LANES]
                    if off:
                        val = pltpu.roll(val, LANES - off, 1)
                else:
                    val = pltpu.roll(block[:, tile : tile + 2 * LANES], 2 * LANES - off, 1)
                    val = val[:, :LANES]
                at = (half * count + h) * LANES
                w_pad[rows, at : at + LANES] = jnp.where(lane < HEAD, val, 0.0).astype(BF16)
            return carry

        lax.fori_loop(0, 8, body, 0)

    wide_heads = HEADS * LANES

    def queries_keys(i):
        rows = slice(i * 512, (i + 1) * 512)

        def body(n, carry):
            cols = pl.ds(pl.multiple_of(n * 512, 512), 512)
            mixed = jnp.dot(norm_buf[rows, :], w_pad[:, cols], preferred_element_type=F32)
            cosine, sin_a, sin_b = cos_buf[rows, :], sin_a_buf[rows, :], sin_b_buf[rows, :]
            outs = []
            for h in range(4):
                val = mixed[:, h * LANES : (h + 1) * LANES]
                val = (
                    val * cosine
                    + pltpu.roll(val, LANES - QUARTER, 1) * sin_a
                    + pltpu.roll(val, QUARTER, 1) * sin_b
                )
                outs.append(val.astype(BF16))
            qk_buf[rows, cols] = jnp.concatenate(outs, axis=1)
            return carry

        lax.fori_loop(0, 2 * wide_heads // 512, body, 0)

    def values(i):
        rows = slice(i * 512, (i + 1) * 512)
        for n in range(wide_heads // 512):
            cols = slice(n * 512, (n + 1) * 512)
            w_cols = slice(2 * wide_heads + n * 512, 2 * wide_heads + (n + 1) * 512)
            mixed = jnp.dot(norm_buf[rows, :], w_pad[:, w_cols], preferred_element_type=F32)
            v_buf[rows, cols] = mixed.astype(BF16)

    exchanged = []

    def attend(j):
        start, area, w_image, owner = image_numbers(grid_ref, owner_ref, j)
        rows = slice(j * image, (j + 1) * image)
        same = lax.broadcasted_iota(jnp.int32, (image, image), 0) == lax.broadcasted_iota(
            jnp.int32, (image, image), 1
        )
        bias = jnp.where((key_buf[j, 0:1, :] > 0.5) | same, 0.0, -1e30)
        best = jnp.full((image, 1), -1e30, F32)
        row, _ = slot_places((image, 1), 0, owner, devices)
        valid = row < area // 4
        for h in range(HEADS):
            lanes = slice(h * LANES, (h + 1) * LANES)
            k_lanes = slice(wide_heads + h * LANES, wide_heads + (h + 1) * LANES)
            scores = lax.dot_general(
                qk_buf[rows, lanes],
                qk_buf[rows, k_lanes],
                (((1,), (1,)), ((), ())),
                preferred_element_type=F32,
            )
            scores = scores * scale + bias
            top = jnp.max(scores, axis=1, keepdims=True)
            best = jnp.maximum(best, top)
            expo = jnp.exp(scores - top)
            total = jnp.sum(expo, axis=1, keepdims=True)
            got = jnp.dot(expo.astype(BF16), v_buf[rows, lanes], preferred_element_type=F32)
            qk_buf[rows, lanes] = (got * jnp.where(valid, 1.0 / total, 0.0)).astype(BF16)
        best = jnp.where(valid, best, -1e30)
        top_ref[j : j + 1, :] = jnp.broadcast_to(
            jnp.max(best, axis=0, keepdims=True), (1, LANES)
        )
        out = lax.dot_general(
            qk_buf[rows, :wide_heads],
            w_pad[:, 3 * wide_heads :],
            (((1,), (1,)), ((), ())),
            preferred_element_type=F32,
        )
        res = out + xs_buf[rows, :].astype(F32)
        turned = pltpu.roll(res, width // 2, 1)
        upper = place.y == 0
        own = jnp.where(upper, res, turned)[:, : width // 2].astype(BF16)
        other = jnp.where(upper, turned, res)[:, : width // 2].astype(BF16)
        at = j * CAP
        for c in range(4):
            hall[c, at : at + CAP, :] = own[c * CAP : (c + 1) * CAP, :]
            hsend[c, at : at + CAP, :] = other[c * CAP : (c + 1) * CAP, :]
        merged_rows = hsend.shape[1]
        exchanged.append(
            wires.copy(
                hsend.at[:, at : at + CAP, :],
                hall.at[:, merged_rows + at : merged_rows + at + CAP, :],
                "y",
            )[1]
        )

    partials = {}

    def project(n):
        if n == 0:
            for c in exchanged:
                c.wait_recv()
        merged_rows = hsend.shape[1]
        cols = slice(n * wide, (n + 1) * wide)
        total = jnp.zeros((2 * merged_rows, wide), F32)
        for c in range(4):
            total = total + jnp.dot(
                hall[c],
                wp_all[c, :, :, :, cols].reshape(width // 2, wide),
                preferred_element_type=F32,
            )
        cown[:, cols] = total[:merged_rows]
        csend[n] = total[merged_rows:].astype(BF16)
        partials[n] = wires.copy(csend.at[n], crecv.at[n], "y")[1]

    def complete(n):
        partials[n].wait_recv()
        merged_rows = hsend.shape[1]
        cols = slice(n * wide, (n + 1) * wide)
        done = cown[:, cols] + crecv[n].astype(F32)
        sq = jnp.sum(done * done, axis=1, keepdims=True)
        if n == 0:
            squares[...] = jnp.broadcast_to(sq, squares.shape)
        else:
            squares[...] += jnp.broadcast_to(sq, squares.shape)
        slots = merged_rows // devices
        out_row = lax.broadcasted_iota(jnp.int32, (merged_rows, merged_rows), 0)
        in_row = lax.broadcasted_iota(jnp.int32, (merged_rows, merged_rows), 1)
        deal = (in_row == (out_row % slots) * devices + out_row // slots).astype(BF16)
        out = jnp.dot(deal, done.astype(BF16), preferred_element_type=F32)
        dealt[:, :, cols] = out.reshape(devices, slots, wide).astype(BF16)

    me = lax.axis_index("dp")
    groups = deal_own.shape[0]
    group_cols = wp_ref.shape[1] // groups

    def deal_out(n):
        cols = slice(n * group_cols, (n + 1) * group_cols)
        pltpu.make_async_copy(
            dealt.at[me, :, cols], routed_ref.at[me, :, cols], deal_own.at[n]
        ).start()

        def give(k, carry):
            to = lax.rem(me + k, devices)
            pltpu.make_async_remote_copy(
                src_ref=dealt.at[to, :, cols],
                dst_ref=routed_ref.at[me, :, cols],
                send_sem=deal_send.at[n],
                recv_sem=deal_recv.at[n],
                device_id=(to,),
                device_id_type=MESH,
            ).start()
            return carry

        lax.fori_loop(1, devices, give, 0)

    def dealt_all():
        for n in range(groups):
            cols = slice(n * group_cols, (n + 1) * group_cols)
            others = routed_ref.at[pl.ds(0, devices - 1), :, cols]
            pltpu.make_async_copy(others, others, deal_recv.at[n]).wait()
            given = dealt.at[pl.ds(0, devices - 1), :, cols]
            pltpu.make_async_copy(given, given, deal_send.at[n]).wait()
            pltpu.make_async_copy(
                dealt.at[me, :, cols], routed_ref.at[me, :, cols], deal_own.at[n]
            ).wait()

    work = {
        0: [lambda: front(0)],
        1: [lambda: front(1)],
        2: [lambda: front(2)],
        3: [lambda: front(3)],
        5: [lambda: spread_heads(0)],
        6: [lambda: queries_keys(0)],
        7: [lambda: spread_heads(1)],
        8: [lambda: values(0), lambda: attend(0)],
        9: [lambda: attend(1)],
        10: [lambda: queries_keys(1)],
        11: [lambda: values(1), lambda: attend(2)],
        12: [lambda: attend(3)],
        15: [lambda: project(0), lambda: project(1), lambda: project(2)],
        16: [lambda: project(3), lambda: complete(0), lambda: complete(1)],
        17: [lambda: project(4), lambda: deal_out(0), lambda: complete(2), lambda: complete(3)],
        18: [lambda: project(5), lambda: deal_out(1), lambda: complete(4)],
        19: [lambda: project(6), lambda: complete(5), lambda: deal_out(2)],
        20: [lambda: project(7), lambda: complete(6), lambda: complete(7), lambda: deal_out(3)],
    }
    when = [
        [0, 1, 2, 3, 4, 5],
        [1, 2, 3, 4, 5, 6],
        [3, 5, 6, 9, 10],
        [5, 7, 8, 11, 12],
        [7, 9, 10, 13, 14],
        [9, 11, 12, 14, 15],
        [10, 11, 13, 15, 16],
        [11, 13, 14, 16, 17],
        [12, 14, 15, 17, 18],
        [13, 15, 16, 18, 19],
    ]
    for step in range(max(work) + 1):
        for steps, pieces in zip(when, chunks):
            for stage, at in enumerate(steps):
                if at == step:
                    for piece in pieces:
                        piece.stage(stage)
        for task in work.get(step, ()):
            task()
    for j in range(images):
        area = image_numbers(grid_ref, owner_ref, j)[1]
        total = jnp.sum(squares[j * CAP : (j + 1) * CAP, :], axis=0, keepdims=True)
        count = (area // 4 * wp_ref.shape[1]).astype(F32)
        rms_ref[j : j + 1, :] = jnp.sqrt(total / count)
    finish(wires)
    dealt_all()


def one_kernel(patches, ln_gain, w_qkv, w_out, w_proj, patch_mask, grid_hw, owners, devices):
    tokens, width = patches.shape
    proj_w = w_proj.shape[1]
    merged = tokens // 4
    images = grid_hw.shape[0]
    vmem = pl.BlockSpec(memory_space=pltpu.VMEM)
    hbm = pl.BlockSpec(memory_space=pl.ANY)
    pad_row = 56
    cols = 4 * HEADS * HEAD
    wide = HEADS * LANES
    p_chunks = 8
    scratch = [
        pltpu.VMEM((pad_row, cols), BF16),
        pltpu.VMEM((4, 2, 2) + w_proj.shape, BF16),
        pltpu.VMEM((width, 4 * wide), BF16),
        pltpu.VMEM((2, 2, 2, pad_row, cols // 2), BF16),
        pltpu.VMEM((tokens, width), BF16),
        pltpu.VMEM((tokens, width), BF16),
        pltpu.VMEM((tokens, 2 * wide), BF16),
        pltpu.VMEM((tokens, wide), BF16),
        pltpu.VMEM((tokens, LANES), F32),
        pltpu.VMEM((tokens, LANES), F32),
        pltpu.VMEM((tokens, LANES), F32),
        pltpu.VMEM((images, 8, 4 * CAP), F32),
        pltpu.VMEM((4, 2 * merged, width // 2), BF16),
        pltpu.VMEM((4, merged, width // 2), BF16),
        pltpu.VMEM((p_chunks, merged, proj_w // p_chunks), BF16),
        pltpu.VMEM((p_chunks, merged, proj_w // p_chunks), BF16),
        pltpu.VMEM((merged, proj_w), F32),
        pltpu.VMEM((merged, LANES), F32),
        pltpu.VMEM((devices, merged // devices, proj_w), BF16),
        pltpu.SemaphoreType.DMA((155,)),
        pltpu.SemaphoreType.DMA((155,)),
        pltpu.SemaphoreType.DMA((14,)),
        pltpu.SemaphoreType.DMA((2,)),
        pltpu.SemaphoreType.DMA((4,)),
        pltpu.SemaphoreType.DMA((4,)),
        pltpu.SemaphoreType.DMA((4,)),
    ]
    return pl.pallas_call(
        functools.partial(whole_kernel, devices),
        out_shape=(
            jax.ShapeDtypeStruct((devices, merged // devices, proj_w), BF16),
            jax.ShapeDtypeStruct((8, LANES), F32),
            jax.ShapeDtypeStruct((8, LANES), F32),
            jax.ShapeDtypeStruct((4, 2, 2, 2, pad_row, cols), BF16),
        ),
        in_specs=[vmem] * 7 + [hbm],
        out_specs=(hbm, vmem, vmem, hbm),
        scratch_shapes=scratch,
        compiler_params=pltpu.CompilerParams(
            collective_id=1, has_side_effects=True, vmem_limit_bytes=63 * 1024 * 1024
        ),
    )(
        patches,
        ln_gain,
        w_qkv,
        w_out.T,
        patch_mask[None, :],
        grid_hw.T,
        owners[None, :],
        w_proj,
    )


def this_slice(patches, ln_gain, w_qkv, w_out, w_proj, seg_ids, patch_mask, grid_hw, owners):
    devices = lax.axis_size("dp")
    images = grid_hw.shape[0]
    routed, rms, top, _ = one_kernel(
        patches, ln_gain, w_qkv, w_out, w_proj, patch_mask, grid_hw, owners, devices
    )
    return routed.reshape(-1, w_proj.shape[1]), rms[:images, 0], top[:images, 0]


def on_device(*args):
    path = this_slice if lax.axis_size("dp") == 32 else any_slice
    return path(*args)


def solution(mesh):
    return jax.shard_map(
        on_device,
        mesh=mesh,
        in_specs=(
            P("dp", None),
            P(),
            P("dp", None),
            P(None, "dp"),
            P("dp", None),
            P("dp"),
            P("dp"),
            P("dp", None),
            P("dp"),
        ),
        out_specs=(P("dp", None), P("dp"), P("dp")),
        check_vma=False,
    )
```
